32 devices in a mesh: row: 8 (over z, x), col: 4 (over y, core).
Axes of the slice: x: 2, y: 2, z: 4, core: 2. Of those that a mesh axis runs over, the one named last changes fastest.
Arguments:
- matrix: float32 [32768, 2048], P('row', 'col'), may hold values from -6 to 6
- leaf_vectors: float32 [3, 32768, 128], P(None, ('row', 'col')), may hold values from -0.09375 to 0.09375
- leaf_factors: float32 [3, 1024, 128], P(None, ('row', 'col')), may hold values from -1.5 to 1.5
- tree_vectors: float32 [3, 1024, 128], P(None, ('row', 'col')), may hold values from -0.5 to 0.5
- tree_factors: float32 [3, 1024, 128], P(None, ('row', 'col')), may hold values from -0.875 to 0.875
Outputs:
- updated: float32 [32768, 2048], P('row', 'col')
The draws below stay inside these ranges and needn't reach their ends.
All inputs are finite; a program needn't handle non-finite values.
Results may differ from the reference program's by a relative error of at most 0.0001.
Values sent between devices are 32-bit elements; how exact they have to be, the bound alone decides.
A program may use at most 128 MiB of HBM per device.

```python
import jax
import jax.numpy as jnp
from jax import lax

B = 128
M_DEV = 4096
TICKS = 3
NROWS = 32768
NCOLS = 2048
LEVELS = 3
N_ROW = 8


def levels(own_key, extent, pieces, least, high):
    gain, own = 1.0, jax.random.fold_in(own_key, 6)
    for dim, blocks in pieces:
        draws = jnp.exp(jax.random.uniform(jax.random.fold_in(own, dim), (blocks,), jnp.float32, least / len(pieces), high / len(pieces)))
        gain = gain * jnp.repeat(draws, extent[dim] // blocks).reshape([-1 if axis == dim else 1 for axis in range(len(extent))])
    return gain


def centred(key, dims, spread, most, pieces=(), held_as=jnp.bfloat16):
    drawn = spread * jax.random.normal(key, dims, jnp.float32)
    if pieces:
        drawn = drawn * levels(key, dims, pieces, -0.22, 0.18)
    return jnp.clip(drawn, -most, most).astype(held_as)


def setup_inputs(seed: int = 0) -> dict:
    key_list = jax.random.split(jax.random.key(seed), 6)
    return {
        "matrix": centred(key_list[0], (NROWS, NCOLS), 1.0, 6.0, ((0, 8), (1, 4)), jnp.float32),
        "leaf_vectors": centred(key_list[1], (TICKS, NROWS, B), M_DEV ** -0.5, 0.09375, ((1, 32),), jnp.float32),
        "leaf_factors": centred(key_list[2], (TICKS, N_ROW * B, B), 0.1, 1.5, ((1, 32),), jnp.float32),
        "tree_vectors": centred(key_list[3], (TICKS, N_ROW * B, B), B ** -0.5, 0.5, ((1, 32),), jnp.float32),
        "tree_factors": centred(key_list[4], (TICKS, N_ROW * B, B), 0.06, 0.875, ((1, 32),), jnp.float32),
    }


def leaf_apply(operands):
    row_block, vectors, factor = operands
    projected = jnp.dot(vectors.T, row_block, precision=lax.Precision.HIGHEST)
    scaled = jnp.dot(jnp.triu(factor).T, projected, precision=lax.Precision.HIGHEST)
    return row_block - jnp.dot(vectors, scaled, precision=lax.Precision.HIGHEST)


def reference(matrix, leaf_vectors, leaf_factors, tree_vectors, tree_factors):
    row_blocks = matrix.reshape(N_ROW, M_DEV, NCOLS)
    hp = lax.Precision.HIGHEST
    for tick_index in range(TICKS):
        vectors = leaf_vectors[tick_index].reshape(N_ROW, M_DEV, B)
        factors = leaf_factors[tick_index].reshape(N_ROW, B, B)
        row_blocks = lax.map(leaf_apply, (row_blocks, vectors, factors))
        top_rows = row_blocks[:, :B, :]
        node_vectors = tree_vectors[tick_index].reshape(N_ROW, B, B)
        node_factors = jnp.triu(tree_factors[tick_index].reshape(N_ROW, B, B))
        for tree_level in range(LEVELS):
            stride = 2 ** tree_level
            upper_ids = jnp.arange(0, N_ROW, 2 * stride)
            lower_ids = upper_ids + stride
            upper_rows = top_rows[upper_ids]
            lower_rows = top_rows[lower_ids]
            vector = node_vectors[lower_ids]
            factor = node_factors[lower_ids]
            summed = upper_rows + jnp.einsum("rab,rac->rbc", vector, lower_rows, precision=hp)
            coupled = jnp.einsum("rab,rac->rbc", factor, summed, precision=hp)
            top_rows = top_rows.at[upper_ids].set(upper_rows - coupled)
            top_rows = top_rows.at[lower_ids].set(lower_rows - jnp.einsum("rab,rbc->rac", vector, coupled, precision=hp))
        row_blocks = row_blocks.at[:, :B, :].set(top_rows)
    return row_blocks.reshape(NROWS, NCOLS)
```

```python
import functools

import jax
import jax.numpy as jnp
from jax import lax
from jax.experimental import pallas as pl
from jax.experimental.pallas import tpu as pltpu
from jax.sharding import PartitionSpec as P

MESH = pl.DeviceIdType.MESH
F32 = jnp.float32
BF16 = jnp.bfloat16
TILE = 512
CHUNKS = 2


def split(x):
    high = x.astype(BF16)
    return high, (x - high.astype(F32)).astype(BF16)


def mm(x, y, contract_x):
    return lax.dot_general(
        x, y, (((contract_x,), (0,)), ((), ())), preferred_element_type=F32
    )


def dot3(x, y, contract_x):
    x_high, x_low = split(x)
    y_high, y_low = split(y)
    return (
        mm(x_high, y_high, contract_x)
        + mm(x_low, y_high, contract_x)
        + mm(x_high, y_low, contract_x)
    )


def upper_triangle(x):
    row = lax.broadcasted_iota(jnp.int32, x.shape, 0)
    col = lax.broadcasted_iota(jnp.int32, x.shape, 1)
    return jnp.where(row <= col, x, 0.0)


def low_bit(mask):
    return mask & -mask


def kernel(
    n_row, n_col,
    a_in, v_in, l_in, y_in, s_in, a,
    v, vc, small, lower_s, top, proj, w_cat, w_low, sent, got,
    a_sem, v_own_sem, v_send, v_recv, small_own, small_send, small_recv,
    s_send, s_recv, x_send, x_recv,
):
    panels, shard, width = v_in.shape
    rows, cols = a_in.shape
    part = l_in.shape[1]
    levels = n_row.bit_length() - 1
    tiles = rows // TILE
    chunk = cols // CHUNKS
    r = lax.axis_index("row")
    c = lax.axis_index("col")

    def partner(mask):
        bits = c
        for bit in range(n_col.bit_length() - 1):
            if mask >> bit & 1:
                bits = bits + (1 << bit) - 2 * (1 << bit) * ((bits // (1 << bit)) % 2)
        return bits

    def row_partner(level):
        step = 1 << level
        return r + step - 2 * step * ((r // step) % 2)

    def block_rows(mask):
        return pl.ds(pl.multiple_of(partner(mask) * shard, shard), shard)

    def part_rows(mask):
        return pl.ds(pl.multiple_of(partner(mask) * part, part), part)

    def a_copy(mask):
        return pltpu.make_async_copy(
            a_in.at[block_rows(mask)], a.at[block_rows(mask)], a_sem.at[mask]
        )

    def v_own(k):
        return pltpu.make_async_copy(v_in.at[k], v.at[k, block_rows(0)], v_own_sem.at[k])

    def v_copy(k, mask):
        bit = low_bit(mask)
        held = mask ^ bit
        source = v_in.at[k] if held == 0 else v.at[k, block_rows(held)]
        return pltpu.make_async_remote_copy(
            src_ref=source,
            dst_ref=v.at[k, block_rows(held)],
            send_sem=v_send.at[k, mask],
            recv_sem=v_recv.at[k, mask],
            device_id={"row": r, "col": partner(bit)},
            device_id_type=MESH,
        )

    def small_local(which, source):
        return pltpu.make_async_copy(
            source, small.at[which, :, part_rows(0)], small_own.at[which]
        )

    def small_copy(which, mask):
        bit = low_bit(mask)
        held = mask ^ bit
        there = small.at[which, :, part_rows(held)]
        return pltpu.make_async_remote_copy(
            src_ref=small_in[which] if held == 0 else there,
            dst_ref=there,
            send_sem=small_send.at[which, mask],
            recv_sem=small_recv.at[which, mask],
            device_id={"row": r, "col": partner(bit)},
            device_id_type=MESH,
        )

    def s_copy(level):
        return pltpu.make_async_remote_copy(
            src_ref=small.at[2],
            dst_ref=lower_s.at[level],
            send_sem=s_send.at[level],
            recv_sem=s_recv.at[level],
            device_id={"row": row_partner(level), "col": c},
            device_id_type=MESH,
        )

    def x_copy(k, level, piece):
        return pltpu.make_async_remote_copy(
            src_ref=sent.at[k, level, piece],
            dst_ref=got.at[k, level, piece],
            send_sem=x_send.at[k, level, piece],
            recv_sem=x_recv.at[k, level, piece],
            device_id={"row": row_partner(level), "col": c},
            device_id_type=MESH,
        )

    def is_lower(level):
        return r % (2 << level) == 1 << level

    def is_upper(level):
        return r % (2 << level) == 0

    def takes_part(level):
        return r % (1 << level) == 0

    masks = range(1, n_col)
    direct = [mask for mask in masks if mask == low_bit(mask)]
    relayed = [mask for mask in masks if mask != low_bit(mask)]
    small_in = (l_in, y_in, s_in)

    for mask in range(n_col):
        a_copy(mask).start()
    for k in range(panels):
        v_own(k).start()
    for which in range(3):
        small_local(which, small_in[which]).start()

    barrier = pltpu.get_barrier_semaphore()
    for mask in masks:
        pl.semaphore_signal(
            barrier, inc=1, device_id={"row": r, "col": partner(mask)}, device_id_type=MESH
        )
    for level in range(levels):
        pl.semaphore_signal(
            barrier, inc=1, device_id={"row": row_partner(level), "col": c}, device_id_type=MESH
        )
    pl.semaphore_wait(barrier, n_col - 1 + levels)

    def start_far(k):
        for mask in masks:
            if mask == low_bit(mask) and mask > 1:
                v_copy(k, mask).start()

    def start_near(k):
        if n_col > 1:
            v_copy(k, 1).start()

    start_near(0)
    start_far(0)
    for which in range(3):
        for mask in direct:
            small_copy(which, mask).start()
    for k in range(1, panels):
        start_near(k)

    def project(k, mask):
        base = partner(mask) * shard

        def step(t, carry):
            at = pl.ds(pl.multiple_of(base + t * TILE, TILE), TILE)
            v_high, v_low = split(v[k, at])
            both = jnp.concatenate([v_high, v_low], axis=1)
            vc[at, :] = both
            a_high, a_low = split(a[at, :])
            out = mm(both, a_high, 0)
            proj[...] += out[:width] + out[width:] + mm(v_high, a_low, 0)
            return carry

        lax.fori_loop(0, shard // TILE, step, 0)

    def update(first, last):
        def step(t, carry):
            at = pl.ds(pl.multiple_of(t * TILE, TILE), TILE)
            both = vc[at, :]
            a[at, :] = a[at, :] - (
                mm(both, w_cat[...], 1) + mm(both[:, :width], w_low[...], 1)
            )
            return carry

        lax.fori_loop(first, last, step, 0)

    def columns(piece):
        return pl.ds(piece * chunk, chunk)

    def send_level(k, level, piece):
        @pl.when(is_lower(level))
        def _():
            sent[k, level, piece] = dot3(small[1, k], top[:, columns(piece)], 0)

        @pl.when(is_upper(level))
        def _():
            sent[k, level, piece] = top[:, columns(piece)]

        @pl.when(takes_part(level))
        def _():
            x_copy(k, level, piece).start()

    def take_level(k, level, piece):
        @pl.when(takes_part(level))
        def _():
            x_copy(k, level, piece).wait_recv()

        @pl.when(is_lower(level))
        def _():
            total = sent[k, level, piece] + got[k, level, piece]
            coupled = dot3(upper_triangle(small[2, k]), total, 0)
            top[:, columns(piece)] -= dot3(small[1, k], coupled, 1)

        @pl.when(is_upper(level))
        def _():
            total = sent[k, level, piece] + got[k, level, piece]
            top[:, columns(piece)] -= dot3(upper_triangle(lower_s[level, k]), total, 0)

    def relay_small(mask):
        for which in range(3):
            small_copy(which, mask).wait_recv()
            bit = 1
            while bit < low_bit(mask):
                small_copy(which, mask | bit).start()
                bit *= 2

    def receive(k, mask):
        v_copy(k, mask).wait_recv()
        bit = 1
        while bit < low_bit(mask):
            v_copy(k, mask | bit).start()
            bit *= 2

    last_direct = n_col // 2
    order = direct + relayed

    proj[...] = jnp.zeros_like(proj)
    a_copy(0).wait()
    v_own(0).wait()
    project(0, 0)

    for k in range(panels):
        for mask in order:
            receive(k, mask)
            if mask == last_direct and k == 0 and panels > 1:
                start_far(k + 1)
            if k == 0:
                a_copy(mask).wait()
                relay_small(mask)
            project(k, mask)
        if k == 0:
            top[...] = a[:width, :]
            for which in range(3):
                small_local(which, small_in[which]).wait()
            for level in range(levels):
                @pl.when(is_lower(level))
                def _():
                    s_copy(level).start()
        else:
            v_high, v_low = split(v[k, pl.ds(0, width)])
            t_high, t_low = split(top[...])
            proj[...] += mm(v_high, t_high, 0) + mm(v_low, t_high, 0) + mm(v_high, t_low, 0)

        w = dot3(upper_triangle(small[0, k]), proj[...], 0)
        w_high, w_small = split(w)
        w_cat[...] = jnp.concatenate([w_high, w_high], axis=0)
        w_low[...] = w_small
        head = vc[pl.ds(0, width), :]
        top[...] -= mm(head, w_cat[...], 1) + mm(head[:, :width], w_low[...], 1)

        for piece in range(CHUNKS):
            send_level(k, 0, piece)
        if k == 0:
            for level in range(levels):
                @pl.when(is_upper(level))
                def _():
                    s_copy(level).wait_recv()
        final = k == panels - 1
        for level in range(levels):
            update(tiles * level // levels, tiles * (level + 1) // levels)
            if level == levels - 1:
                if not final:
                    a[:width, :] = jnp.zeros((width, cols), F32)
                    proj[...] = jnp.zeros_like(proj)
                    v_own(k + 1).wait()
                    project(k + 1, 0)
            for piece in range(CHUNKS):
                take_level(k, level, piece)
                if level + 1 < levels:
                    send_level(k, level + 1, piece)
            if level == 0 and k + 2 < panels:
                start_far(k + 2)

    a[:width, :] = top[...]

    for k in range(panels):
        for mask in masks:
            v_copy(k, mask).wait_send()
    for which in range(3):
        for mask in masks:
            small_copy(which, mask).wait_send()
    for level in range(levels):
        @pl.when(is_lower(level))
        def _():
            s_copy(level).wait_send()

        @pl.when(takes_part(level))
        def _():
            for k in range(panels):
                for piece in range(CHUNKS):
                    x_copy(k, level, piece).wait_send()


def local(n_row, n_col, matrix, leaf_vectors, leaf_factors, tree_vectors, tree_factors):
    rows, cols = matrix.shape
    panels, shard, width = leaf_vectors.shape
    levels = n_row.bit_length() - 1
    chunk = cols // CHUNKS
    anywhere = pl.BlockSpec(memory_space=pl.ANY)
    dma = pltpu.SemaphoreType.DMA
    return pl.pallas_call(
        functools.partial(kernel, n_row, n_col),
        out_shape=pltpu.VMEM((rows, cols), F32),
        in_specs=[anywhere] * 5,
        out_specs=pl.BlockSpec(memory_space=pltpu.VMEM),
        scratch_shapes=[
            pltpu.VMEM((panels, rows, width), F32),
            pltpu.VMEM((rows, 2 * width), BF16),
            pltpu.VMEM((3, panels, width, width), F32),
            pltpu.VMEM((levels, panels, width, width), F32),
            pltpu.VMEM((width, cols), F32),
            pltpu.VMEM((width, cols), F32),
            pltpu.VMEM((2 * width, cols), BF16),
            pltpu.VMEM((width, cols), BF16),
            pltpu.VMEM((panels, levels, CHUNKS, width, chunk), F32),
            pltpu.VMEM((panels, levels, CHUNKS, width, chunk), F32),
            dma((n_col,)),
            dma((panels,)),
            dma((panels, n_col)),
            dma((panels, n_col)),
            dma((3,)),
            dma((3, n_col)),
            dma((3, n_col)),
            dma((levels,)),
            dma((levels,)),
            dma((panels, levels, CHUNKS)),
            dma((panels, levels, CHUNKS)),
        ],
        compiler_params=pltpu.CompilerParams(
            collective_id=0, has_side_effects=True, vmem_limit_bytes=44 << 20
        ),
    )(matrix, leaf_vectors, leaf_factors, tree_vectors, tree_factors)


def solution(mesh):
    placed = (
        P("row", "col"),
        P(None, ("row", "col"), None),
        P(None, ("row", "col"), None),
        P(None, ("row", "col"), None),
        P(None, ("row", "col"), None),
    )
    return jax.shard_map(
        functools.partial(local, mesh.shape["row"], mesh.shape["col"]),
        mesh=mesh, in_specs=placed, out_specs=P("row", "col"), check_vma=False,
    )
```

```python
import functools

import jax
import jax.numpy as jnp
from jax import lax
from jax.experimental import pallas as pl
from jax.experimental.pallas import tpu as pltpu
from jax.sharding import PartitionSpec as P

MESH = pl.DeviceIdType.MESH
F32 = jnp.float32
BF16 = jnp.bfloat16
TILE = 512
PIECE = 256
CHUNK = 128


def split(x):
    high = x.astype(BF16)
    return high, (x - high.astype(F32)).astype(BF16)


def mm(x, y, contract_x):
    return lax.dot_general(
        x, y, (((contract_x,), (0,)), ((), ())), preferred_element_type=F32
    )


def dot3(x, y, contract_x):
    x_high, x_low = x if isinstance(x, tuple) else split(x)
    y_high, y_low = y if isinstance(y, tuple) else split(y)
    return (
        mm(x_high, y_high, contract_x)
        + mm(x_low, y_high, contract_x)
        + mm(x_high, y_low, contract_x)
    )


def upper_triangle(x):
    row = lax.broadcasted_iota(jnp.int32, x.shape, 0)
    col = lax.broadcasted_iota(jnp.int32, x.shape, 1)
    return jnp.where(row <= col, x, 0.0)


def low_bit(mask):
    return mask & -mask


def kernel(
    n_row, n_col,
    a_in, v_in, l_in, y_in, s_in, a,
    v, vc, small, node, pair_s, top, carry, q, w_all, xb, zb, sent, got, back,
    a_sem, v_own_sem, v_send, v_recv, small_own, small_send, small_recv,
    node_send, node_recv, s_send, s_recv, x_send, x_recv, z_send, z_recv,
    t_send, t_recv, b_send, b_recv,
):
    panels, shard, width = v_in.shape
    rows, cols = a_in.shape
    part = l_in.shape[1]
    levels = n_row.bit_length() - 1
    tiles = rows // TILE
    pieces = shard // PIECE
    chunks = cols // CHUNK
    half = chunks // 2
    r = lax.axis_index("row")
    c = lax.axis_index("col")
    odd = r % 2
    node_of = r - odd
    is_even = odd == 0
    is_odd = odd == 1
    groups = [(0, 1)] + ([(1, panels - 1)] if panels > 1 else [])

    def partner(mask):
        bits = c
        for bit in range(n_col.bit_length() - 1):
            if mask >> bit & 1:
                bits = bits + (1 << bit) - 2 * (1 << bit) * ((bits // (1 << bit)) % 2)
        return bits

    def row_partner(level):
        step = 1 << level
        return r + step - 2 * step * ((r // step) % 2)

    def block_start(mask):
        return pl.multiple_of(partner(mask) * shard, shard)

    def part_rows(mask):
        return pl.ds(pl.multiple_of(partner(mask) * part, part), part)

    def to_row(level, source, there, send, recv):
        return pltpu.make_async_remote_copy(
            src_ref=source, dst_ref=there, send_sem=send, recv_sem=recv,
            device_id={"row": row_partner(level), "col": c}, device_id_type=MESH,
        )

    def to_col(bit, source, there, send, recv):
        return pltpu.make_async_remote_copy(
            src_ref=source, dst_ref=there, send_sem=send, recv_sem=recv,
            device_id={"row": r, "col": partner(bit)}, device_id_type=MESH,
        )

    def a_copy(mask):
        at = pl.ds(block_start(mask), shard)
        return pltpu.make_async_copy(a_in.at[at], a.at[at], a_sem.at[mask])

    def v_own(k):
        at = pl.ds(block_start(0), shard)
        return pltpu.make_async_copy(v_in.at[k], v.at[k, at], v_own_sem.at[k])

    def cuts(mask):
        return [(0, shard)] if mask == 1 else [(p * PIECE, PIECE) for p in range(pieces)]

    def v_copy(k, mask, p):
        first, size = cuts(mask)[p]
        bit = low_bit(mask)
        held = mask ^ bit
        there = v.at[k, pl.ds(block_start(held) + first, size)]
        source = v_in.at[k, pl.ds(first, size)] if held == 0 else there
        return to_col(bit, source, there, v_send.at[k, mask, p], v_recv.at[k, mask, p])

    small_in = (l_in, y_in, s_in)

    def small_local(which, g):
        k = pl.ds(*groups[g])
        return pltpu.make_async_copy(
            small_in[which].at[k], small.at[which, k, part_rows(0)], small_own.at[which, g]
        )

    def small_copy(which, g, mask):
        bit = low_bit(mask)
        held = mask ^ bit
        k = pl.ds(*groups[g])
        there = small.at[which, k, part_rows(held)]
        return to_col(
            bit, small_in[which].at[k] if held == 0 else there, there,
            small_send.at[which, g, mask], small_recv.at[which, g, mask],
        )

    def node_copy(g):
        k = pl.ds(*groups[g])
        return to_row(
            0, small.at[pl.ds(1, 2), k], node.at[:, k], node_send.at[g], node_recv.at[g]
        )

    def s_copy(level, g):
        k = pl.ds(*groups[g])
        source = small.at[2, k] if level == 0 else node.at[1, k]
        return to_row(
            level, source, pair_s.at[level, k], s_send.at[level, g], s_recv.at[level, g]
        )

    def x_copy(k, chunk):
        there = xb.at[k, chunk]
        return to_row(0, there, there, x_send.at[k, chunk], x_recv.at[k, chunk])

    def z_copy(k, chunk):
        there = zb.at[k, chunk]
        return to_row(0, there, there, z_send.at[k, chunk], z_recv.at[k, chunk])

    def t_copy(k, level, p):
        return to_row(
            level, sent.at[k, level, p], got.at[k, level, p],
            t_send.at[k, level, p], t_recv.at[k, level, p],
        )

    def b_copy(k, p):
        there = back.at[k, p]
        return to_row(0, there, there, b_send.at[k, p], b_recv.at[k, p])

    def is_lower(level):
        return node_of % (2 << level) == 1 << level

    def is_upper(level):
        return node_of % (2 << level) == 0

    def takes_part(level):
        return node_of % (1 << level) == 0

    def ends_at(level):
        return takes_part(level) if level == levels - 1 else is_lower(level)

    masks = range(1, n_col)
    near = [mask for mask in masks if mask == 1]
    far = [mask for mask in masks if mask > 1 and mask == low_bit(mask)]
    relayed = [mask for mask in masks if mask != low_bit(mask)]

    a_copy(0).start()
    v_own(0).start()
    for mask in masks:
        a_copy(mask).start()
    for g in range(len(groups)):
        for which in range(3):
            small_local(which, g).start()
    for k in range(1, panels):
        v_own(k).start()

    barrier = pltpu.get_barrier_semaphore()
    for mask in masks:
        pl.semaphore_signal(
            barrier, inc=1, device_id={"row": r, "col": partner(mask)}, device_id_type=MESH
        )
    for level in range(levels):
        pl.semaphore_signal(
            barrier, inc=1, device_id={"row": row_partner(level), "col": c}, device_id_type=MESH
        )
    pl.semaphore_wait(barrier, n_col - 1 + levels)

    for k in range(panels):
        if k < len(groups):
            for mask in far + near:
                for which in range(3):
                    small_copy(which, k, mask).start()
        for mask in far + near:
            for p in range(len(cuts(mask))):
                v_copy(k, mask, p).start()

    def project(k, mask, first, last):
        base = block_start(mask)
        wide = cols + k * width

        def step(t, carry_in):
            start = pl.multiple_of(base + t * TILE, TILE)
            at = pl.ds(start, TILE)
            row = lax.broadcasted_iota(jnp.int32, (TILE, width), 0) + start
            high, low = split(jnp.where(row >= width, v[k, at], 0.0))
            both = jnp.concatenate([high, low], axis=1)
            a_high, a_low = split(a[at, :])
            before = [vc[at, 2 * width * j:2 * width * (j + 1)] for j in range(k)]
            right = jnp.concatenate([a_high] + [x[:, :width] for x in before], axis=1)
            right_low = jnp.concatenate([a_low] + [x[:, width:] for x in before], axis=1)
            vc[at, 2 * width * k:2 * width * (k + 1)] = both
            out = mm(both, right, 0)
            q[k, :, :wide] += out[:width] + out[width:] + mm(high, right_low, 0)
            return carry_in

        lax.fori_loop(first, last, step, 0)

    def update(first, last):
        def step(t, carry_in):
            at = pl.ds(pl.multiple_of(t * TILE, TILE), TILE)
            left = jnp.concatenate(
                [vc[at, :]]
                + [vc[at, 2 * width * k:2 * width * k + width] for k in range(panels)],
                axis=1,
            )
            a[at, :] = a[at, :] - mm(left, w_all[...], 1)
            return carry_in

        lax.fori_loop(first, last, step, 0)

    def leaf(k):
        head = split(v[k, pl.ds(0, width)])
        x = top[...]
        proj = q[k, :, :cols] + dot3(head, x, 0)
        for j in range(k):
            w_j = (
                w_all[2 * width * j:2 * width * j + width, :],
                w_all[2 * width * panels + width * j:2 * width * panels + width * (j + 1), :],
            )
            proj -= dot3(q[k, :, cols + width * j:cols + width * (j + 1)], w_j, 1)
        high, low = split(dot3(upper_triangle(small[0, k]), proj, 0))
        w_all[2 * width * k:2 * width * k + width, :] = high
        w_all[2 * width * k + width:2 * width * (k + 1), :] = high
        w_all[2 * width * panels + width * k:2 * width * panels + width * (k + 1), :] = low
        top[...] = x - dot3(head, (high, low), 1)

    def columns(chunk):
        return pl.ds(chunk * CHUNK, CHUNK)

    def send_first(k):
        @pl.when(is_even)
        def _():
            for chunk in list(range(half, chunks)) + list(range(half)):
                xb[k, chunk] = top[:, columns(chunk)]
                x_copy(k, chunk).start()

        @pl.when(is_odd)
        def _():
            z = dot3(small[1, k], top[...], 0)
            for chunk in range(chunks):
                zb[k, chunk] = z[:, chunk * CHUNK:(chunk + 1) * CHUNK]
                if chunk < half:
                    z_copy(k, chunk).start()

    def couple(level, k, total):
        return dot3(upper_triangle(pair_s[level, k]), total, 0)

    def finish_own(k, chunk, coupled):
        top[:, columns(chunk)] -= dot3(small[1, k], coupled, 1)

    def take_first(k, p):
        @pl.when(is_even)
        def _():
            z_copy(k, p).wait_recv()
            x = xb[k, p]
            carry[p] = x - couple(0, k, x + zb[k, p])

        @pl.when(is_odd)
        def _():
            x_copy(k, half + p).wait_recv()
            x = xb[k, half + p]
            coupled = couple(0, k, x + zb[k, half + p])
            carry[p] = x - coupled
            finish_own(k, half + p, coupled)

    def finish_first(k):
        @pl.when(is_odd)
        def _():
            for chunk in range(half):
                x_copy(k, chunk).wait_recv()
                finish_own(k, chunk, couple(0, k, xb[k, chunk] + zb[k, chunk]))

    def send_level(k, level, p):
        @pl.when(is_lower(level))
        def _():
            sent[k, level, p] = dot3(node[0, k], carry[p], 0)

        @pl.when(is_upper(level))
        def _():
            sent[k, level, p] = carry[p]

        @pl.when(takes_part(level))
        def _():
            t_copy(k, level, p).start()

    def take_level(k, level, p):
        @pl.when(takes_part(level))
        def _():
            t_copy(k, level, p).wait_recv()
            coupled = couple(level, k, sent[k, level, p] + got[k, level, p])

            @pl.when(is_lower(level))
            def _():
                carry[p] -= dot3(node[0, k], coupled, 1)

            @pl.when(is_upper(level))
            def _():
                carry[p] -= coupled

    def end_level(k, level, p):
        @pl.when(ends_at(level) & is_even)
        def _():
            top[:, columns(p)] = carry[p]

        @pl.when(ends_at(level) & is_odd)
        def _():
            back[k, p] = carry[p]
            b_copy(k, p).start()

    def take_back(k):
        @pl.when(is_even)
        def _():
            for p in range(half):
                b_copy(k, p).wait_recv()
                top[:, columns(half + p)] = back[k, p]

    def pass_on(mask):
        bit = 1
        while bit < low_bit(mask):
            yield mask | bit
            bit *= 2

    def small_far(g):
        for mask in near + far:
            for which in range(3):
                small_copy(which, g, mask).wait_recv()
                for onward in pass_on(mask):
                    small_copy(which, g, onward).start()

    def small_rest(g):
        for mask in relayed:
            for which in range(3):
                small_copy(which, g, mask).wait_recv()
                for onward in pass_on(mask):
                    small_copy(which, g, onward).start()
        for which in range(3):
            small_local(which, g).wait()
        k = pl.ds(*groups[g])

        @pl.when(is_odd)
        def _():
            s_copy(0, g).start()
            pair_s[0, k] = small[2, k]

        @pl.when(is_even)
        def _():
            node[:, k] = small[pl.ds(1, 2), k]

        @pl.when(is_even & (r > 0))
        def _():
            node_copy(g).start()

    def node_rest(g):
        @pl.when(is_odd & (r > 1))
        def _():
            node_copy(g).wait_recv()

        k = pl.ds(*groups[g])
        for level in range(1, levels):
            @pl.when(is_lower(level))
            def _():
                s_copy(level, g).start()
                pair_s[level, k] = node[1, k]

    def pair_rest(g, level):
        mine = is_even if level == 0 else is_upper(level)

        @pl.when(mine)
        def _():
            s_copy(level, g).wait_recv()

    def receive(k, mask, p):
        v_copy(k, mask, p).wait_recv()
        for onward in pass_on(mask):
            v_copy(k, onward, p).start()

    steps = shard // TILE
    per_step = TILE // PIECE

    def far_step(k, t):
        for mask in far + relayed:
            for p in range(per_step * t, per_step * (t + 1)):
                receive(k, mask, p)
            if k == 0 and t == 0:
                a_copy(mask).wait()
            project(k, mask, t, t + 1)

    def near_all(k):
        v_own(k).wait()
        project(k, 0, 0, steps)
        for mask in near:
            if k == 0:
                a_copy(mask).wait()
            receive(k, mask, 0)
            project(k, mask, 0, steps)

    q[...] = jnp.zeros_like(q)
    a_copy(0).wait()
    near_all(0)
    small_far(0)
    for k in range(1, panels):
        near_all(k)
        if k == 1:
            small_rest(0)
    if panels == 1:
        small_rest(0)
    node_rest(0)
    for t in range(steps):
        far_step(0, t)
    top[...] = a[:width, :]
    for level in range(levels):
        pair_rest(0, level)

    for k in range(panels):
        final = k == panels - 1
        more = k == 0 and len(groups) > 1
        gaps = levels + 1

        def fill(gap):
            if final:
                update(tiles * gap // gaps, tiles * (gap + 1) // gaps)

        leaf(k)
        send_first(k)
        fill(0)
        if more:
            small_far(1)
        if k == 1:
            pair_rest(1, 0)
        for p in range(half):
            take_first(k, p)
            if levels > 1:
                send_level(k, 1, p)
            else:
                end_level(k, 0, p)
        finish_first(k)
        if more:
            small_rest(1)
        for level in range(1, levels):
            fill(level)
            if k == 1 and level == 1:
                for other in range(1, levels):
                    pair_rest(1, other)
            if not final and level == levels - 1:
                for t in range(steps - 1):
                    far_step(k + 1, t)
            for p in range(half):
                take_level(k, level, p)
                if level + 1 < levels:
                    send_level(k, level + 1, p)
                end_level(k, level, p)
        fill(levels)
        if more:
            node_rest(1)
        if not final:
            for t in range(steps - 1 if levels > 1 else 0, steps):
                far_step(k + 1, t)
        take_back(k)

    a[:width, :] = top[...]

    for k in range(panels):
        for mask in masks:
            for p in range(len(cuts(mask))):
                v_copy(k, mask, p).wait_send()
    for g in range(len(groups)):
        for which in range(3):
            for mask in masks:
                small_copy(which, g, mask).wait_send()

        @pl.when(is_odd)
        def _():
            s_copy(0, g).wait_send()

        @pl.when(is_even & (r > 0))
        def _():
            node_copy(g).wait_send()

        for level in range(1, levels):
            @pl.when(is_lower(level))
            def _():
                s_copy(level, g).wait_send()

    for k in range(panels):
        @pl.when(is_even)
        def _():
            for chunk in range(chunks):
                x_copy(k, chunk).wait_send()

        @pl.when(is_odd)
        def _():
            for p in range(half):
                z_copy(k, p).wait_send()
                b_copy(k, p).wait_send()

        for level in range(1, levels):
            @pl.when(takes_part(level))
            def _():
                for p in range(half):
                    t_copy(k, level, p).wait_send()


def local(n_row, n_col, matrix, leaf_vectors, leaf_factors, tree_vectors, tree_factors):
    rows, cols = matrix.shape
    panels, shard, width = leaf_vectors.shape
    levels = n_row.bit_length() - 1
    pieces = shard // PIECE
    chunks = cols // CHUNK
    half = chunks // 2
    groups = min(panels, 2)
    dma = pltpu.SemaphoreType.DMA
    vmem = pltpu.VMEM
    return pl.pallas_call(
        functools.partial(kernel, n_row, n_col),
        out_shape=pltpu.VMEM((rows, cols), F32),
        in_specs=[pl.BlockSpec(memory_space=pltpu.HBM)] * 5,
        out_specs=pl.BlockSpec(memory_space=pltpu.VMEM),
        scratch_shapes=[
            vmem((panels, rows, width), F32),
            vmem((rows, 2 * width * panels), BF16),
            vmem((3, panels, width, width), F32),
            vmem((2, panels, width, width), F32),
            vmem((levels, panels, width, width), F32),
            vmem((width, cols), F32),
            vmem((half, width, CHUNK), F32),
            vmem((panels, width, cols + width * (panels - 1)), F32),
            vmem((3 * width * panels, cols), BF16),
            vmem((panels, chunks, width, CHUNK), F32),
            vmem((panels, chunks, width, CHUNK), F32),
            vmem((panels, levels, half, width, CHUNK), F32),
            vmem((panels, levels, half, width, CHUNK), F32),
            vmem((panels, half, width, CHUNK), F32),
            dma((n_col,)),
            dma((panels,)),
            dma((panels, n_col, pieces)),
            dma((panels, n_col, pieces)),
            dma((3, groups)),
            dma((3, groups, n_col)),
            dma((3, groups, n_col)),
            dma((groups,)),
            dma((groups,)),
            dma((levels, groups)),
            dma((levels, groups)),
            dma((panels, chunks)),
            dma((panels, chunks)),
            dma((panels, half)),
            dma((panels, half)),
            dma((panels, levels, half)),
            dma((panels, levels, half)),
            dma((panels, half)),
            dma((panels, half)),
        ],
        compiler_params=pltpu.CompilerParams(
            collective_id=0, has_side_effects=True, vmem_limit_bytes=48 << 20
        ),
    )(matrix, leaf_vectors, leaf_factors, tree_vectors, tree_factors)


def solution(mesh):
    placed = (
        P("row", "col"),
        P(None, ("row", "col"), None),
        P(None, ("row", "col"), None),
        P(None, ("row", "col"), None),
        P(None, ("row", "col"), None),
    )
    return jax.shard_map(
        functools.partial(local, mesh.shape["row"], mesh.shape["col"]),
        mesh=mesh, in_specs=placed, out_specs=P("row", "col"), check_vma=False,
    )
```

```python
import functools

import jax
import jax.numpy as jnp
from jax import lax
from jax.experimental import pallas as pl
from jax.experimental.pallas import tpu as pltpu
from jax.sharding import PartitionSpec as P

MESH = pl.DeviceIdType.MESH
F32 = jnp.float32
BF16 = jnp.bfloat16
TILE = 512
PIECE = 256
CHUNK = 128


def split(x):
    high = x.astype(BF16)
    return high, (x - high.astype(F32)).astype(BF16)


def mm(x, y, contract_x):
    return lax.dot_general(
        x, y, (((contract_x,), (0,)), ((), ())), preferred_element_type=F32
    )


def dot3(x, y, contract_x):
    x_high, x_low = x if isinstance(x, tuple) else split(x)
    y_high, y_low = y if isinstance(y, tuple) else split(y)
    return (
        mm(x_high, y_high, contract_x)
        + mm(x_low, y_high, contract_x)
        + mm(x_high, y_low, contract_x)
    )


def upper_triangle(x):
    row = lax.broadcasted_iota(jnp.int32, x.shape, 0)
    col = lax.broadcasted_iota(jnp.int32, x.shape, 1)
    return jnp.where(row <= col, x, 0.0)


def low_bit(mask):
    return mask & -mask


def kernel(
    n_row, n_col,
    a_in, v_in, l_in, y_in, s_in, a,
    v, vc, small, pair_ys, pair_s, pair_vb, top_out, tops, carry, q, w_all,
    r_out, r_got, w_out, w_got, sent, got, b_out, b_got,
    a_sem, v_own_sem, v_send, v_recv, small_own, small_send, small_recv,
    ys_send, ys_recv, s_send, s_recv, vb_send, vb_recv, top_send, top_recv,
    r_send, r_recv, w_send, w_recv, t_send, t_recv, b_send, b_recv,
):
    panels, shard, width = v_in.shape
    rows, cols = a_in.shape
    part = l_in.shape[1]
    levels = n_row.bit_length() - 1
    tiles = rows // TILE
    pieces = shard // PIECE
    span = cols // 2
    half = span // CHUNK
    r = lax.axis_index("row")
    c = lax.axis_index("col")
    odd = r % 2
    other = 1 - odd
    node_of = r - odd
    is_even = odd == 0
    is_odd = odd == 1
    groups = [(0, 1)] + ([(1, panels - 1)] if panels > 1 else [])

    def partner(mask):
        bits = c
        for bit in range(n_col.bit_length() - 1):
            if mask >> bit & 1:
                bits = bits + (1 << bit) - 2 * (1 << bit) * ((bits // (1 << bit)) % 2)
        return bits

    def row_partner(level):
        step = 1 << level
        return r + step - 2 * step * ((r // step) % 2)

    def block_start(mask):
        return pl.multiple_of(partner(mask) * shard, shard)

    def part_rows(mask):
        return pl.ds(pl.multiple_of(partner(mask) * part, part), part)

    def to_row(level, source, there, send, recv):
        return pltpu.make_async_remote_copy(
            src_ref=source, dst_ref=there, send_sem=send, recv_sem=recv,
            device_id={"row": row_partner(level), "col": c}, device_id_type=MESH,
        )

    def to_col(bit, source, there, send, recv):
        return pltpu.make_async_remote_copy(
            src_ref=source, dst_ref=there, send_sem=send, recv_sem=recv,
            device_id={"row": r, "col": partner(bit)}, device_id_type=MESH,
        )

    def a_copy(mask):
        at = pl.ds(block_start(mask), shard)
        return pltpu.make_async_copy(a_in.at[at], a.at[at], a_sem.at[mask])

    def v_own(k):
        at = pl.ds(block_start(0), shard)
        return pltpu.make_async_copy(v_in.at[k], v.at[k, at], v_own_sem.at[k])

    def cuts(mask):
        return [(0, shard)] if mask == 1 else [(p * PIECE, PIECE) for p in range(pieces)]

    def v_copy(k, mask, p):
        first, size = cuts(mask)[p]
        bit = low_bit(mask)
        held = mask ^ bit
        there = v.at[k, pl.ds(block_start(held) + first, size)]
        source = v_in.at[k, pl.ds(first, size)] if held == 0 else there
        return to_col(bit, source, there, v_send.at[k, mask, p], v_recv.at[k, mask, p])

    small_in = (l_in, y_in, s_in)

    def small_local(which, g):
        k = pl.ds(*groups[g])
        return pltpu.make_async_copy(
            small_in[which].at[k], small.at[which, k, part_rows(0)], small_own.at[which, g]
        )

    def small_copy(which, g, mask):
        bit = low_bit(mask)
        held = mask ^ bit
        k = pl.ds(*groups[g])
        there = small.at[which, k, part_rows(held)]
        return to_col(
            bit, small_in[which].at[k] if held == 0 else there, there,
            small_send.at[which, g, mask], small_recv.at[which, g, mask],
        )

    def ys_copy(g):
        k = pl.ds(*groups[g])
        return to_row(
            0, small.at[pl.ds(1, 2), k], pair_ys.at[odd, :, k], ys_send.at[g], ys_recv.at[g]
        )

    def s_copy(level, g):
        k = pl.ds(*groups[g])
        return to_row(
            level, pair_ys.at[0, 1, k], pair_s.at[level, k],
            s_send.at[level, g], s_recv.at[level, g],
        )

    def vb_copy(k):
        there = pair_vb.at[odd, k]
        return to_row(0, there, there, vb_send.at[k], vb_recv.at[k])

    def top_copy():
        return to_row(0, top_out.at[other], tops.at[odd], top_send, top_recv)

    def r_copy(k):
        return to_row(0, r_out.at[k, other], r_got.at[k], r_send.at[k], r_recv.at[k])

    def w_copy(k):
        return to_row(0, w_out.at[k], w_got.at[k], w_send.at[k], w_recv.at[k])

    def t_copy(k, level, p):
        return to_row(
            level, sent.at[k, level, p], got.at[k, level, p],
            t_send.at[k, level, p], t_recv.at[k, level, p],
        )

    def b_copy(p):
        return to_row(0, b_out.at[p], b_got.at[p], b_send.at[p], b_recv.at[p])

    def is_lower(level):
        return node_of % (2 << level) == 1 << level

    def is_upper(level):
        return node_of % (2 << level) == 0

    def takes_part(level):
        return node_of % (1 << level) == 0

    def ends_at(level):
        return takes_part(level) if level == levels - 1 else is_lower(level)

    masks = range(1, n_col)
    near = [mask for mask in masks if mask == 1]
    far = [mask for mask in masks if mask > 1 and mask == low_bit(mask)]
    relayed = [mask for mask in masks if mask != low_bit(mask)]

    a_copy(0).start()
    v_own(0).start()
    for mask in masks:
        a_copy(mask).start()
    for g in range(len(groups)):
        for which in range(3):
            small_local(which, g).start()
    for k in range(1, panels):
        v_own(k).start()

    barrier = pltpu.get_barrier_semaphore()
    for mask in masks:
        pl.semaphore_signal(
            barrier, inc=1, device_id={"row": r, "col": partner(mask)}, device_id_type=MESH
        )
    for level in range(levels):
        pl.semaphore_signal(
            barrier, inc=1, device_id={"row": row_partner(level), "col": c}, device_id_type=MESH
        )
    pl.semaphore_wait(barrier, n_col - 1 + levels)

    for k in range(panels):
        if k < len(groups):
            for mask in far + near:
                for which in range(3):
                    small_copy(which, k, mask).start()
        for mask in far + near:
            for p in range(len(cuts(mask))):
                v_copy(k, mask, p).start()

    def project(k, mask, first, last):
        base = block_start(mask)
        wide = cols + k * width

        def step(t, carry_in):
            start = pl.multiple_of(base + t * TILE, TILE)
            at = pl.ds(start, TILE)
            row = lax.broadcasted_iota(jnp.int32, (TILE, width), 0) + start
            high, low = split(jnp.where(row >= width, v[k, at], 0.0))
            both = jnp.concatenate([high, low], axis=1)
            a_high, a_low = split(a[at, :])
            before = [vc[at, 2 * width * j:2 * width * (j + 1)] for j in range(k)]
            right = jnp.concatenate([a_high] + [x[:, :width] for x in before], axis=1)
            right_low = jnp.concatenate([a_low] + [x[:, width:] for x in before], axis=1)
            vc[at, 2 * width * k:2 * width * (k + 1)] = both
            out = mm(both, right, 0)
            q[k, :, :wide] += out[:width] + out[width:] + mm(high, right_low, 0)
            return carry_in

        lax.fori_loop(first, last, step, 0)

    def update(ks, first, last):
        terms = [(2 * width * k, 2 * width) for k in ks]
        low_terms = [2 * width * panels + width * k for k in ks]

        def step(t, carry_in):
            at = pl.ds(pl.multiple_of(t * TILE, TILE), TILE)
            left = jnp.concatenate(
                [vc[at, first_col:first_col + size] for first_col, size in terms]
                + [vc[at, first_col:first_col + width] for first_col, size in terms],
                axis=1,
            )
            right = jnp.concatenate([
                jnp.concatenate(
                    [w_all[h, row:row + size, :] for row, size in terms]
                    + [w_all[h, row:row + width, :] for row in low_terms],
                    axis=0,
                )
                for h in range(2)
            ], axis=1)
            a[at, :] = a[at, :] - mm(left, right, 1)
            return carry_in

        lax.fori_loop(first, last, step, 0)

    def make_vb(k):
        head = v[k, pl.ds(0, width)]
        pair_vb[odd, k, 0] = head
        pair_vb[odd, k, 1] = dot3(head, upper_triangle(small[0, k]), 1)
        vb_copy(k).start()

    def set_w(k, h, w):
        high, low = split(w)
        w_all[h, 2 * width * k:2 * width * k + width, :] = high
        w_all[h, 2 * width * k + width:2 * width * (k + 1), :] = high
        w_all[h, 2 * width * panels + width * k:2 * width * panels + width * (k + 1), :] = low

    def make_r(k):
        proj = q[k, :, :cols]
        for j in range(k):
            w_j = tuple(
                jnp.concatenate([w_all[h, row:row + width, :] for h in range(2)], axis=1)
                for row in (2 * width * j, 2 * width * panels + width * j)
            )
            proj -= dot3(q[k, :, cols + width * j:cols + width * (j + 1)], w_j, 1)
        out = dot3(upper_triangle(small[0, k]), proj, 0)
        r_out[k, 0] = out[:, :span]
        r_out[k, 1] = out[:, span:]
        r_copy(k).start()

    def leaf(k):
        vb_copy(k).wait_recv()
        r_copy(k).wait_recv()
        x = tops[odd]
        w = r_out[k, odd] + dot3(pair_vb[odd, k, 1], x, 0)
        x_other = tops[other]
        w_other = r_got[k] + dot3(pair_vb[other, k, 1], x_other, 0)
        w_out[k] = w_other
        w_copy(k).start()
        set_w(k, odd, w)
        tops[odd] = x - dot3(pair_vb[odd, k, 0], w, 1)
        tops[other] = x_other - dot3(pair_vb[other, k, 0], w_other, 1)

    def take_w(k):
        w_copy(k).wait_recv()
        set_w(k, other, w_got[k])

    def couple(s, total):
        return dot3(upper_triangle(s), total, 0)

    def first_level(k, final):
        lower = split(pair_ys[1, 0, k])
        x = tops[0]
        x_lower = tops[1]
        coupled = couple(pair_ys[1, 1, k], x + dot3(lower, x_lower, 0))
        upper = x - coupled
        for p in range(half):
            carry[p] = upper[:, p * CHUNK:(p + 1) * CHUNK]
            if levels > 1:
                send_level(k, 1, p)
            else:
                end_level(final, 0, p)
        x_lower = x_lower - dot3(lower, coupled, 1)
        tops[1] = x_lower

        if final:
            @pl.when(is_even)
            def _():
                for p in range(half):
                    b_out[p] = x_lower[:, p * CHUNK:(p + 1) * CHUNK]
                    b_copy(p).start()

    def send_level(k, level, p):
        @pl.when(is_lower(level))
        def _():
            sent[k, level, p] = dot3(pair_ys[0, 0, k], carry[p], 0)

        @pl.when(is_upper(level))
        def _():
            sent[k, level, p] = carry[p]

        @pl.when(takes_part(level))
        def _():
            t_copy(k, level, p).start()

    def take_level(k, level, p):
        @pl.when(takes_part(level))
        def _():
            t_copy(k, level, p).wait_recv()
            coupled = couple(pair_s[level, k], sent[k, level, p] + got[k, level, p])

            @pl.when(is_lower(level))
            def _():
                carry[p] -= dot3(pair_ys[0, 0, k], coupled, 1)

            @pl.when(is_upper(level))
            def _():
                carry[p] -= coupled

    def end_level(final, level, p):
        if final:
            @pl.when(ends_at(level) & is_odd)
            def _():
                b_out[p] = carry[p]
                b_copy(p).start()

    def pass_on(mask):
        bit = 1
        while bit < low_bit(mask):
            yield mask | bit
            bit *= 2

    def small_far(g):
        for mask in near + far:
            for which in range(3):
                small_copy(which, g, mask).wait_recv()
                for onward in pass_on(mask):
                    small_copy(which, g, onward).start()

    def small_rest(g):
        for mask in relayed:
            for which in range(3):
                small_copy(which, g, mask).wait_recv()
                for onward in pass_on(mask):
                    small_copy(which, g, onward).start()
        for which in range(3):
            small_local(which, g).wait()
        k = pl.ds(*groups[g])
        ys_copy(g).start()
        pair_ys[odd, :, k] = small[pl.ds(1, 2), k]

    def node_rest(g):
        ys_copy(g).wait_recv()
        k = pl.ds(*groups[g])
        for level in range(1, levels):
            @pl.when(is_lower(level))
            def _():
                s_copy(level, g).start()
                pair_s[level, k] = pair_ys[0, 1, k]

    def pair_rest(g):
        for level in range(1, levels):
            @pl.when(is_upper(level))
            def _():
                s_copy(level, g).wait_recv()

    def receive(k, mask, p):
        v_copy(k, mask, p).wait_recv()
        for onward in pass_on(mask):
            v_copy(k, onward, p).start()

    steps = shard // TILE
    per_step = TILE // PIECE

    def far_step(k, t):
        for mask in far + relayed:
            for p in range(per_step * t, per_step * (t + 1)):
                receive(k, mask, p)
            project(k, mask, t, t + 1)

    def near_all(k):
        v_own(k).wait()
        project(k, 0, 0, steps)
        for mask in near:
            receive(k, mask, 0)
            project(k, mask, 0, steps)

    def far_all(k, t):
        far_step(k, t)
        if t == 0:
            make_vb(k)
        if t == steps - 1:
            make_r(k)

    q[...] = jnp.zeros_like(q)
    for mask in range(n_col):
        a_copy(mask).wait()
    top_out[0] = a[:width, :span]
    top_out[1] = a[:width, span:]
    top_copy().start()
    tops[odd] = top_out[odd]
    near_all(0)
    small_far(0)
    for k in range(1, panels):
        near_all(k)
        if k == 1:
            small_rest(0)
    if panels == 1:
        small_rest(0)
    node_rest(0)
    for t in range(steps):
        far_all(0, t)
    top_copy().wait_recv()
    pair_rest(0)

    for k in range(panels):
        final = k == panels - 1
        more = k == 0 and len(groups) > 1
        if final and k > 0:
            update(range(k), 0, tiles)
        leaf(k)
        first_level(k, final)
        if more:
            small_far(1)
            small_rest(1)
        if not final:
            for t in range(steps - 1):
                far_all(k + 1, t)
        if final and levels > 1:
            take_w(k)
        for level in range(1, levels):
            if level == levels - 1:
                if not final:
                    take_w(k)
                    far_all(k + 1, steps - 1)
                else:
                    update([k], 0, tiles // 2)
            for p in range(half):
                take_level(k, level, p)
                if level + 1 < levels:
                    send_level(k, level + 1, p)
                end_level(final, level, p)
        if levels == 1:
            take_w(k)
            if not final:
                far_all(k + 1, steps - 1)
        for p in range(half):
            tops[0, :, p * CHUNK:(p + 1) * CHUNK] = carry[p]
        if more:
            node_rest(1)
            pair_rest(1)

    update([panels - 1], tiles // 2 if levels > 1 else 0, tiles)
    for p in range(half):
        b_copy(p).wait_recv()

    @pl.when(is_even)
    def _():
        a[:width, :span] = tops[0]
        for p in range(half):
            a[:width, span + p * CHUNK:span + (p + 1) * CHUNK] = b_got[p]

    @pl.when(is_odd)
    def _():
        a[:width, span:] = tops[1]
        for p in range(half):
            a[:width, p * CHUNK:(p + 1) * CHUNK] = b_got[p]

    for k in range(panels):
        for mask in masks:
            for p in range(len(cuts(mask))):
                v_copy(k, mask, p).wait_send()
    for g in range(len(groups)):
        for which in range(3):
            for mask in masks:
                small_copy(which, g, mask).wait_send()

        ys_copy(g).wait_send()
        for level in range(1, levels):
            @pl.when(is_lower(level))
            def _():
                s_copy(level, g).wait_send()

    top_copy().wait_send()
    for k in range(panels):
        vb_copy(k).wait_send()
        r_copy(k).wait_send()
        w_copy(k).wait_send()
        for level in range(1, levels):
            @pl.when(takes_part(level))
            def _():
                for p in range(half):
                    t_copy(k, level, p).wait_send()
    for p in range(half):
        b_copy(p).wait_send()


def local(n_row, n_col, matrix, leaf_vectors, leaf_factors, tree_vectors, tree_factors):
    rows, cols = matrix.shape
    panels, shard, width = leaf_vectors.shape
    levels = n_row.bit_length() - 1
    pieces = shard // PIECE
    span = cols // 2
    half = span // CHUNK
    groups = min(panels, 2)
    dma = pltpu.SemaphoreType.DMA
    vmem = pltpu.VMEM
    return pl.pallas_call(
        functools.partial(kernel, n_row, n_col),
        out_shape=pltpu.VMEM((rows, cols), F32),
        in_specs=[pl.BlockSpec(memory_space=pltpu.HBM)] * 5,
        out_specs=pl.BlockSpec(memory_space=pltpu.VMEM),
        scratch_shapes=[
            vmem((panels, rows, width), F32),
            vmem((rows, 2 * width * panels), BF16),
            vmem((3, panels, width, width), F32),
            vmem((2, 2, panels, width, width), F32),
            vmem((levels, panels, width, width), F32),
            vmem((2, panels, 2, width, width), F32),
            vmem((2, width, span), F32),
            vmem((2, width, span), F32),
            vmem((half, width, CHUNK), F32),
            vmem((panels, width, cols + width * (panels - 1)), F32),
            vmem((2, 3 * width * panels, span), BF16),
            vmem((panels, 2, width, span), F32),
            vmem((panels, width, span), F32),
            vmem((panels, width, span), F32),
            vmem((panels, width, span), F32),
            vmem((panels, levels, half, width, CHUNK), F32),
            vmem((panels, levels, half, width, CHUNK), F32),
            vmem((half, width, CHUNK), F32),
            vmem((half, width, CHUNK), F32),
            dma((n_col,)),
            dma((panels,)),
            dma((panels, n_col, pieces)),
            dma((panels, n_col, pieces)),
            dma((3, groups)),
            dma((3, groups, n_col)),
            dma((3, groups, n_col)),
            dma((groups,)),
            dma((groups,)),
            dma((levels, groups)),
            dma((levels, groups)),
            dma((panels,)),
            dma((panels,)),
            dma(()),
            dma(()),
            dma((panels,)),
            dma((panels,)),
            dma((panels,)),
            dma((panels,)),
            dma((panels, levels, half)),
            dma((panels, levels, half)),
            dma((half,)),
            dma((half,)),
        ],
        compiler_params=pltpu.CompilerParams(
            collective_id=0, has_side_effects=True, vmem_limit_bytes=48 << 20
        ),
    )(matrix, leaf_vectors, leaf_factors, tree_vectors, tree_factors)


def solution(mesh):
    placed = (
        P("row", "col"),
        P(None, ("row", "col"), None),
        P(None, ("row", "col"), None),
        P(None, ("row", "col"), None),
        P(None, ("row", "col"), None),
    )
    return jax.shard_map(
        functools.partial(local, mesh.shape["row"], mesh.shape["col"]),
        mesh=mesh, in_specs=placed, out_specs=P("row", "col"), check_vma=False,
    )
```

```python
import functools

import jax
import jax.numpy as jnp
from jax import lax
from jax.experimental import pallas as pl
from jax.experimental.pallas import tpu as pltpu
from jax.sharding import PartitionSpec as P

MESH = pl.DeviceIdType.MESH
F32 = jnp.float32
BF16 = jnp.bfloat16
TILE = 512
UPDATE = 1024
PIECE = 512
CHUNK = 128


def split(x):
    high = x.astype(BF16)
    return high, (x - high.astype(F32)).astype(BF16)


def mm(x, y, contract_x):
    return lax.dot_general(
        x, y, (((contract_x,), (0,)), ((), ())), preferred_element_type=F32
    )


def dot3(x, y, contract_x):
    x_high, x_low = x if isinstance(x, tuple) else split(x)
    y_high, y_low = y if isinstance(y, tuple) else split(y)
    return (
        mm(x_high, y_high, contract_x)
        + mm(x_low, y_high, contract_x)
        + mm(x_high, y_low, contract_x)
    )


def upper_triangle(x):
    row = lax.broadcasted_iota(jnp.int32, x.shape, 0)
    col = lax.broadcasted_iota(jnp.int32, x.shape, 1)
    return jnp.where(row <= col, x, 0.0)


def low_bit(mask):
    return mask & -mask


def kernel(
    n_row, n_col,
    a_in, v_in, l_in, y_in, s_in, a,
    v, vc, small, pair_ys, pair_s, pair_vb, top_out, tops, carry, q, w_all,
    r_all, r_got, w_pair, w_out, w_got, pre_w, pre_x, pre_z, step_m,
    sent, got, b_out, b_got,
    a_sem, v_own_sem, v_send, v_recv, small_own, small_send, small_recv,
    ys_send, ys_recv, s_send, s_recv, vb_send, vb_recv, top_send, top_recv,
    r_send, r_recv, w_send, w_recv, t_send, t_recv, b_send, b_recv,
):
    panels, shard, width = v_in.shape
    rows, cols = a_in.shape
    part = l_in.shape[1]
    levels = n_row.bit_length() - 1
    tiles = rows // UPDATE
    pieces = shard // PIECE
    span = cols // 2
    half = span // CHUNK
    r = lax.axis_index("row")
    c = lax.axis_index("col")
    odd = r % 2
    other = 1 - odd
    node_of = r - odd
    is_even = odd == 0
    is_odd = odd == 1
    groups = [(k, 1) for k in range(panels)]

    def partner(mask):
        bits = c
        for bit in range(n_col.bit_length() - 1):
            if mask >> bit & 1:
                bits = bits + (1 << bit) - 2 * (1 << bit) * ((bits // (1 << bit)) % 2)
        return bits

    def row_partner(level):
        step = 1 << level
        return r + step - 2 * step * ((r // step) % 2)

    def block_start(mask):
        return pl.multiple_of(partner(mask) * shard, shard)

    def part_rows(mask):
        return pl.ds(pl.multiple_of(partner(mask) * part, part), part)

    def to_row(level, source, there, send, recv):
        return pltpu.make_async_remote_copy(
            src_ref=source, dst_ref=there, send_sem=send, recv_sem=recv,
            device_id={"row": row_partner(level), "col": c}, device_id_type=MESH,
        )

    def to_col(bit, source, there, send, recv):
        return pltpu.make_async_remote_copy(
            src_ref=source, dst_ref=there, send_sem=send, recv_sem=recv,
            device_id={"row": r, "col": partner(bit)}, device_id_type=MESH,
        )

    def a_copy(mask):
        at = pl.ds(block_start(mask), shard)
        return pltpu.make_async_copy(a_in.at[at], a.at[at], a_sem.at[mask])

    def v_own(k):
        at = pl.ds(block_start(0), shard)
        return pltpu.make_async_copy(v_in.at[k], v.at[k, at], v_own_sem.at[k])

    def cuts(mask):
        return [(0, shard)] if mask == 1 else [(p * PIECE, PIECE) for p in range(pieces)]

    def v_copy(k, mask, p):
        first, size = cuts(mask)[p]
        bit = low_bit(mask)
        held = mask ^ bit
        there = v.at[k, pl.ds(block_start(held) + first, size)]
        source = v_in.at[k, pl.ds(first, size)] if held == 0 else there
        return to_col(bit, source, there, v_send.at[k, mask, p], v_recv.at[k, mask, p])

    small_in = (l_in, y_in, s_in)

    def small_local(which, g):
        k = pl.ds(*groups[g])
        return pltpu.make_async_copy(
            small_in[which].at[k], small.at[which, k, part_rows(0)], small_own.at[which, g]
        )

    def small_copy(which, g, mask):
        bit = low_bit(mask)
        held = mask ^ bit
        k = pl.ds(*groups[g])
        there = small.at[which, k, part_rows(held)]
        return to_col(
            bit, small_in[which].at[k] if held == 0 else there, there,
            small_send.at[which, g, mask], small_recv.at[which, g, mask],
        )

    def ys_copy(k):
        return to_row(
            0, small.at[pl.ds(1, 2), k], pair_ys.at[odd, :, k], ys_send.at[k], ys_recv.at[k]
        )

    def s_copy(level, k):
        return to_row(
            level, pair_ys.at[0, 1, k], pair_s.at[level, k],
            s_send.at[level, k], s_recv.at[level, k],
        )

    def vb_copy(k):
        there = pair_vb.at[odd, k]
        return to_row(0, there, there, vb_send.at[k], vb_recv.at[k])

    def top_copy():
        return to_row(0, top_out.at[other], tops.at[odd], top_send, top_recv)

    def r_copy(k, p):
        return to_row(
            0, r_all.at[k, other, p], r_got.at[k, p], r_send.at[k, p], r_recv.at[k, p]
        )

    def w_copy(k):
        return to_row(0, w_out.at[k], w_got.at[k], w_send.at[k], w_recv.at[k])

    def t_copy(k, level, p):
        return to_row(
            level, sent.at[k, level, p], got.at[k, level, p],
            t_send.at[k, level, p], t_recv.at[k, level, p],
        )

    def b_copy(p):
        return to_row(0, b_out.at[p], b_got.at[p], b_send.at[p], b_recv.at[p])

    def is_lower(level):
        return node_of % (2 << level) == 1 << level

    def is_upper(level):
        return node_of % (2 << level) == 0

    def takes_part(level):
        return node_of % (1 << level) == 0

    def ends_at(level):
        return takes_part(level) if level == levels - 1 else is_lower(level)

    masks = range(1, n_col)
    near = [mask for mask in masks if mask == 1]
    far = [mask for mask in masks if mask > 1 and mask == low_bit(mask)]
    relayed = [mask for mask in masks if mask != low_bit(mask)]

    a_copy(0).start()
    v_own(0).start()
    for mask in masks:
        a_copy(mask).start()
    for g in range(len(groups)):
        for which in range(3):
            small_local(which, g).start()
    for k in range(1, panels):
        v_own(k).start()

    barrier = pltpu.get_barrier_semaphore()
    for mask in masks:
        pl.semaphore_signal(
            barrier, inc=1, device_id={"row": r, "col": partner(mask)}, device_id_type=MESH
        )
    for level in range(levels):
        pl.semaphore_signal(
            barrier, inc=1, device_id={"row": row_partner(level), "col": c}, device_id_type=MESH
        )
    pl.semaphore_wait(barrier, n_col - 1 + levels)

    for k in range(panels):
        if k < len(groups):
            for mask in far + near:
                for which in range(3):
                    small_copy(which, k, mask).start()
        for mask in far + near:
            for p in range(len(cuts(mask))):
                v_copy(k, mask, p).start()

    def project(k, mask, first, last):
        base = block_start(mask)
        wide = cols + k * width

        def step(t, carry_in):
            start = pl.multiple_of(base + t * TILE, TILE)
            at = pl.ds(start, TILE)
            row = lax.broadcasted_iota(jnp.int32, (TILE, width), 0) + start
            high, low = split(jnp.where(row >= width, v[k, at], 0.0))
            both = jnp.concatenate([high, low], axis=1)
            a_high, a_low = split(a[at, :])
            before = [vc[at, 2 * width * j:2 * width * (j + 1)] for j in range(k)]
            right = jnp.concatenate([a_high] + [x[:, :width] for x in before], axis=1)
            right_low = jnp.concatenate([a_low] + [x[:, width:] for x in before], axis=1)
            vc[at, 2 * width * k:2 * width * (k + 1)] = both
            out = mm(both, right, 0)
            q[k, :, :wide] += out[:width] + out[width:] + mm(high, right_low, 0)
            return carry_in

        lax.fori_loop(first, last, step, 0)

    def update(ks, first, last):
        terms = [(2 * width * k, 2 * width) for k in ks]
        low_terms = [2 * width * panels + width * k for k in ks]

        def step(t, carry_in):
            at = pl.ds(pl.multiple_of(t * UPDATE, UPDATE), UPDATE)
            left = jnp.concatenate(
                [vc[at, first_col:first_col + size] for first_col, size in terms]
                + [vc[at, first_col:first_col + width] for first_col, size in terms],
                axis=1,
            )
            right = jnp.concatenate([
                jnp.concatenate(
                    [w_all[h, row:row + size, :] for row, size in terms]
                    + [w_all[h, row:row + width, :] for row in low_terms],
                    axis=0,
                )
                for h in range(2)
            ], axis=1)
            a[at, :] = a[at, :] - mm(left, right, 1)
            return carry_in

        lax.fori_loop(first, last, step, 0)

    def make_vb(k):
        head = v[k, pl.ds(0, width)]
        pair_vb[odd, k, 0] = head
        pair_vb[odd, k, 1] = dot3(head, upper_triangle(small[0, k]), 1)
        vb_copy(k).start()

    def set_w(k, h, w):
        high, low = split(w)
        w_all[h, 2 * width * k:2 * width * k + width, :] = high
        w_all[h, 2 * width * k + width:2 * width * (k + 1), :] = high
        w_all[h, 2 * width * panels + width * k:2 * width * panels + width * (k + 1), :] = low

    def make_r(k):
        proj = q[k, :, :cols]
        for j in range(k):
            w_j = tuple(
                jnp.concatenate([w_all[h, row:row + width, :] for h in range(2)], axis=1)
                for row in (2 * width * j, 2 * width * panels + width * j)
            )
            proj -= dot3(q[k, :, cols + width * j:cols + width * (j + 1)], w_j, 1)
        out = dot3(upper_triangle(small[0, k]), proj, 0)
        for p in range(half):
            for h in range(2):
                at = h * span + p * CHUNK
                r_all[k, h, p] = out[:, at:at + CHUNK]
            r_copy(k, p).start()

    def plan(k):
        vb_copy(k).wait_recv()
        head = pair_vb[0, k, 0]
        lower = dot3(pair_ys[1, 0, k], pair_vb[1, k, 0], 0)
        coupled = couple(pair_ys[1, 1, k], jnp.concatenate([head, lower], axis=1))
        both = jnp.concatenate([head, jnp.zeros_like(head)], axis=1) - coupled
        step_m[k, 0] = both
        step_m[k, 1] = dot3(pair_ys[0, 0, k], both, 0)

    def before(k):
        x = tops[0]
        x_lower = tops[1]
        pre_w[0] = dot3(pair_vb[0, k, 1], x, 0)
        pre_w[1] = dot3(pair_vb[1, k, 1], x_lower, 0)
        after = x - couple(pair_ys[1, 1, k], x + dot3(pair_ys[1, 0, k], x_lower, 0))
        pre_x[...] = after
        if levels > 1:
            @pl.when(is_lower(1))
            def _():
                pre_z[...] = dot3(pair_ys[0, 0, k], after, 0)

    def take_w(k):
        w_copy(k).wait_recv()
        set_w(k, other, w_got[k])

    def couple(s, total):
        return dot3(upper_triangle(s), total, 0)

    def piece(p):
        return slice(p * CHUNK, (p + 1) * CHUNK)

    def first_level(k, final):
        for p in range(half):
            r_copy(k, p).wait_recv()
            w_pair[odd, p] = r_all[k, odd, p] + pre_w[odd, :, piece(p)]
            w_pair[other, p] = r_got[k, p] + pre_w[other, :, piece(p)]
            w = split(jnp.concatenate([w_pair[0, p], w_pair[1, p]], axis=0))
            if levels == 1:
                carry[p] = pre_x[:, piece(p)] - dot3(step_m[k, 0], w, 1)
                end_level(final, 0, p)
                continue

            @pl.when(is_lower(1))
            def _():
                sent[k, 1, p] = pre_z[:, piece(p)] - dot3(step_m[k, 1], w, 1)
                t_copy(k, 1, p).start()
                carry[p] = pre_x[:, piece(p)] - dot3(step_m[k, 0], w, 1)

            @pl.when(is_upper(1))
            def _():
                upper = pre_x[:, piece(p)] - dot3(step_m[k, 0], w, 1)
                carry[p] = upper
                sent[k, 1, p] = upper
                t_copy(k, 1, p).start()

        for p in range(half):
            w_out[k, :, piece(p)] = w_pair[other, p]
        w_copy(k).start()

        def joined(ref, *index):
            return jnp.concatenate([ref[(*index, p)] for p in range(half)], axis=1)

        set_w(k, odd, joined(w_pair, odd))
        x = tops[0] - dot3(pair_vb[0, k, 0], joined(w_pair, 0), 1)
        x_lower = tops[1] - dot3(pair_vb[1, k, 0], joined(w_pair, 1), 1)
        x_lower -= dot3(pair_ys[1, 0, k], x - joined(carry), 1)
        tops[1] = x_lower

        if final:
            @pl.when(is_even)
            def _():
                for p in range(half):
                    b_out[p] = x_lower[:, piece(p)]
                    b_copy(p).start()

    def send_level(k, level, p):
        @pl.when(is_lower(level))
        def _():
            sent[k, level, p] = dot3(pair_ys[0, 0, k], carry[p], 0)

        @pl.when(is_upper(level))
        def _():
            sent[k, level, p] = carry[p]

        @pl.when(takes_part(level))
        def _():
            t_copy(k, level, p).start()

    def take_level(k, level, p):
        @pl.when(takes_part(level))
        def _():
            t_copy(k, level, p).wait_recv()
            coupled = couple(pair_s[level, k], sent[k, level, p] + got[k, level, p])

            @pl.when(is_lower(level))
            def _():
                carry[p] -= dot3(pair_ys[0, 0, k], coupled, 1)

            @pl.when(is_upper(level))
            def _():
                carry[p] -= coupled

    def end_level(final, level, p):
        if final:
            @pl.when(ends_at(level) & is_odd)
            def _():
                b_out[p] = carry[p]
                b_copy(p).start()

    def pass_on(mask):
        bit = 1
        while bit < low_bit(mask):
            yield mask | bit
            bit *= 2

    def small_far(g):
        for mask in near + far:
            for which in range(3):
                small_copy(which, g, mask).wait_recv()
                for onward in pass_on(mask):
                    small_copy(which, g, onward).start()

    def small_rest(g):
        for mask in relayed:
            for which in range(3):
                small_copy(which, g, mask).wait_recv()
                for onward in pass_on(mask):
                    small_copy(which, g, onward).start()
        for which in range(3):
            small_local(which, g).wait()

    def share_ys(k):
        ys_copy(k).start()
        pair_ys[odd, :, k] = small[pl.ds(1, 2), k]

    def node_rest(k):
        ys_copy(k).wait_recv()
        for level in range(1, levels):
            @pl.when(is_lower(level))
            def _():
                s_copy(level, k).start()
                pair_s[level, k] = pair_ys[0, 1, k]

    def pair_rest(k):
        for level in range(1, levels):
            @pl.when(is_upper(level))
            def _():
                s_copy(level, k).wait_recv()

    def receive(k, mask, p):
        v_copy(k, mask, p).wait_recv()
        for onward in pass_on(mask):
            v_copy(k, onward, p).start()

    steps = shard // TILE
    per_step = TILE // PIECE

    def far_step(k, t):
        for mask in far + relayed:
            for p in range(per_step * t, per_step * (t + 1)):
                receive(k, mask, p)
            project(k, mask, t, t + 1)

    def near_all(k):
        v_own(k).wait()
        project(k, 0, 0, steps)
        for mask in near:
            receive(k, mask, 0)
            project(k, mask, 0, steps)

    def far_all(k, t):
        far_step(k, t)
        if t == 0:
            make_vb(k)
        if t == steps - 1:
            make_r(k)

    q[...] = jnp.zeros_like(q)
    for mask in range(n_col):
        a_copy(mask).wait()
    top_out[0] = a[:width, :span]
    top_out[1] = a[:width, span:]
    top_copy().start()
    tops[odd] = top_out[odd]
    near_all(0)
    small_far(0)
    small_rest(0)
    share_ys(0)
    for k in range(1, panels):
        near_all(k)
    for t in range(steps):
        far_all(0, t)
    node_rest(0)
    top_copy().wait_recv()
    plan(0)

    for k in range(panels):
        final = k == panels - 1

        def next_vectors(first, last):
            if not final:
                for t in range(first, last):
                    far_all(k + 1, t)

        before(k)
        first_level(k, final)
        if not final:
            small_far(k + 1)
            small_rest(k + 1)
            share_ys(k + 1)
        next_vectors(0, steps - 1)
        if final and k > 0:
            update(range(k), 0, tiles)
        pair_rest(k)
        for level in range(1, levels):
            for p in range(half):
                take_level(k, level, p)
                if level + 1 < levels:
                    send_level(k, level + 1, p)
                end_level(final, level, p)
            if level == 1:
                take_w(k)
                next_vectors(steps - 1, steps)
                if not final:
                    node_rest(k + 1)
                    plan(k + 1)
                else:
                    update([k], 0, tiles)
        if levels == 1:
            take_w(k)
            next_vectors(steps - 1, steps)
            if not final:
                node_rest(k + 1)
                plan(k + 1)
            else:
                update([k], 0, tiles)
        for p in range(half):
            tops[0, :, piece(p)] = carry[p]

    for p in range(half):
        b_copy(p).wait_recv()

    @pl.when(is_even)
    def _():
        a[:width, :span] = tops[0]
        for p in range(half):
            a[:width, span + p * CHUNK:span + (p + 1) * CHUNK] = b_got[p]

    @pl.when(is_odd)
    def _():
        a[:width, span:] = tops[1]
        for p in range(half):
            a[:width, p * CHUNK:(p + 1) * CHUNK] = b_got[p]

    for k in range(panels):
        for mask in masks:
            for p in range(len(cuts(mask))):
                v_copy(k, mask, p).wait_send()
    for g in range(len(groups)):
        for which in range(3):
            for mask in masks:
                small_copy(which, g, mask).wait_send()


    top_copy().wait_send()
    for k in range(panels):
        ys_copy(k).wait_send()
        for level in range(1, levels):
            @pl.when(is_lower(level))
            def _():
                s_copy(level, k).wait_send()

        vb_copy(k).wait_send()
        for p in range(half):
            r_copy(k, p).wait_send()
        w_copy(k).wait_send()
        for level in range(1, levels):
            @pl.when(takes_part(level))
            def _():
                for p in range(half):
                    t_copy(k, level, p).wait_send()
    for p in range(half):
        b_copy(p).wait_send()


def local(n_row, n_col, matrix, leaf_vectors, leaf_factors, tree_vectors, tree_factors):
    rows, cols = matrix.shape
    panels, shard, width = leaf_vectors.shape
    levels = n_row.bit_length() - 1
    pieces = shard // PIECE
    span = cols // 2
    half = span // CHUNK
    groups = panels
    dma = pltpu.SemaphoreType.DMA
    vmem = pltpu.VMEM
    return pl.pallas_call(
        functools.partial(kernel, n_row, n_col),
        out_shape=pltpu.VMEM((rows, cols), F32),
        in_specs=[pl.BlockSpec(memory_space=pltpu.HBM)] * 5,
        out_specs=pl.BlockSpec(memory_space=pltpu.VMEM),
        scratch_shapes=[
            vmem((panels, rows, width), F32),
            vmem((rows, 2 * width * panels), BF16),
            vmem((3, panels, width, width), F32),
            vmem((2, 2, panels, width, width), F32),
            vmem((levels, panels, width, width), F32),
            vmem((2, panels, 2, width, width), F32),
            vmem((2, width, span), F32),
            vmem((2, width, span), F32),
            vmem((half, width, CHUNK), F32),
            vmem((panels, width, cols + width * (panels - 1)), F32),
            vmem((2, 3 * width * panels, span), BF16),
            vmem((panels, 2, half, width, CHUNK), F32),
            vmem((panels, half, width, CHUNK), F32),
            vmem((2, half, width, CHUNK), F32),
            vmem((panels, width, span), F32),
            vmem((panels, width, span), F32),
            vmem((2, width, span), F32),
            vmem((width, span), F32),
            vmem((width, span), F32),
            vmem((panels, 2, width, 2 * width), F32),
            vmem((panels, levels, half, width, CHUNK), F32),
            vmem((panels, levels, half, width, CHUNK), F32),
            vmem((half, width, CHUNK), F32),
            vmem((half, width, CHUNK), F32),
            dma((n_col,)),
            dma((panels,)),
            dma((panels, n_col, pieces)),
            dma((panels, n_col, pieces)),
            dma((3, groups)),
            dma((3, groups, n_col)),
            dma((3, groups, n_col)),
            dma((panels,)),
            dma((panels,)),
            dma((levels, panels)),
            dma((levels, panels)),
            dma((panels,)),
            dma((panels,)),
            dma(()),
            dma(()),
            dma((panels, half)),
            dma((panels, half)),
            dma((panels,)),
            dma((panels,)),
            dma((panels, levels, half)),
            dma((panels, levels, half)),
            dma((half,)),
            dma((half,)),
        ],
        compiler_params=pltpu.CompilerParams(
            collective_id=0, has_side_effects=True, vmem_limit_bytes=48 << 20
        ),
    )(matrix, leaf_vectors, leaf_factors, tree_vectors, tree_factors)


def solution(mesh):
    placed = (
        P("row", "col"),
        P(None, ("row", "col"), None),
        P(None, ("row", "col"), None),
        P(None, ("row", "col"), None),
        P(None, ("row", "col"), None),
    )
    return jax.shard_map(
        functools.partial(local, mesh.shape["row"], mesh.shape["col"]),
        mesh=mesh, in_specs=placed, out_specs=P("row", "col"), check_vma=False,
    )
```

```python
import functools

import jax
import jax.numpy as jnp
from jax import lax
from jax.experimental import pallas as pl
from jax.experimental.pallas import tpu as pltpu
from jax.sharding import PartitionSpec as P

MESH = pl.DeviceIdType.MESH
F32 = jnp.float32
BF16 = jnp.bfloat16
TILE = 512
UPDATE = 1024
PIECE = 512
CHUNK = 128


def split(x):
    high = x.astype(BF16)
    return high, (x - high.astype(F32)).astype(BF16)


def mm(x, y, contract_x):
    return lax.dot_general(
        x, y, (((contract_x,), (0,)), ((), ())), preferred_element_type=F32
    )


def dot3(x, y, contract_x):
    x_high, x_low = x if isinstance(x, tuple) else split(x)
    y_high, y_low = y if isinstance(y, tuple) else split(y)
    return (
        mm(x_high, y_high, contract_x)
        + mm(x_low, y_high, contract_x)
        + mm(x_high, y_low, contract_x)
    )


def upper_triangle(x):
    row = lax.broadcasted_iota(jnp.int32, x.shape, 0)
    col = lax.broadcasted_iota(jnp.int32, x.shape, 1)
    return jnp.where(row <= col, x, 0.0)


def low_bit(mask):
    return mask & -mask


def kernel(
    n_row, n_col,
    a_in, v_in, l_in, y_in, s_in, a,
    v, vc, small, pair_ys, pair_s, pair_vb, top_out, tops, carry, q, w_all,
    r_all, r_got, w_pair, w_out, w_got, pre_w, pre_x, pre_z, step_m,
    sent, got, b_out, b_got,
    a_sem, v_own_sem, v_send, v_recv, small_own, small_send, small_recv,
    ys_send, ys_recv, s_send, s_recv, vb_send, vb_recv, top_send, top_recv,
    r_send, r_recv, w_send, w_recv, t_send, t_recv, b_send, b_recv,
):
    panels, shard, width = v_in.shape
    rows, cols = a_in.shape
    part = l_in.shape[1]
    levels = n_row.bit_length() - 1
    tiles = rows // UPDATE
    pieces = shard // PIECE
    span = cols // 2
    half = span // CHUNK
    r = lax.axis_index("row")
    c = lax.axis_index("col")
    odd = r % 2
    other = 1 - odd
    node_of = r - odd
    is_even = odd == 0
    is_odd = odd == 1
    groups = [(k, 1) for k in range(panels)]

    def partner(mask):
        bits = c
        for bit in range(n_col.bit_length() - 1):
            if mask >> bit & 1:
                bits = bits + (1 << bit) - 2 * (1 << bit) * ((bits // (1 << bit)) % 2)
        return bits

    def row_partner(level):
        step = 1 << level
        return r + step - 2 * step * ((r // step) % 2)

    def block_start(mask):
        return pl.multiple_of(partner(mask) * shard, shard)

    def part_rows(mask):
        return pl.ds(pl.multiple_of(partner(mask) * part, part), part)

    def to_row(level, source, there, send, recv):
        return pltpu.make_async_remote_copy(
            src_ref=source, dst_ref=there, send_sem=send, recv_sem=recv,
            device_id={"row": row_partner(level), "col": c}, device_id_type=MESH,
        )

    def to_col(bit, source, there, send, recv):
        return pltpu.make_async_remote_copy(
            src_ref=source, dst_ref=there, send_sem=send, recv_sem=recv,
            device_id={"row": r, "col": partner(bit)}, device_id_type=MESH,
        )

    def a_copy(mask):
        at = pl.ds(block_start(mask), shard)
        return pltpu.make_async_copy(a_in.at[at], a.at[at], a_sem.at[mask])

    def v_own(k):
        at = pl.ds(block_start(0), shard)
        return pltpu.make_async_copy(v_in.at[k], v.at[k, at], v_own_sem.at[k])

    def cuts(mask):
        return [(0, shard)] if mask == 1 else [(p * PIECE, PIECE) for p in range(pieces)]

    def v_copy(k, mask, p):
        first, size = cuts(mask)[p]
        bit = low_bit(mask)
        held = mask ^ bit
        there = v.at[k, pl.ds(block_start(held) + first, size)]
        source = v_in.at[k, pl.ds(first, size)] if held == 0 else there
        return to_col(bit, source, there, v_send.at[k, mask, p], v_recv.at[k, mask, p])

    small_in = (l_in, y_in, s_in)

    def small_local(which, g):
        k = pl.ds(*groups[g])
        return pltpu.make_async_copy(
            small_in[which].at[k], small.at[which, k, part_rows(0)], small_own.at[which, g]
        )

    def small_copy(which, g, mask):
        bit = low_bit(mask)
        held = mask ^ bit
        k = pl.ds(*groups[g])
        there = small.at[which, k, part_rows(held)]
        return to_col(
            bit, small_in[which].at[k] if held == 0 else there, there,
            small_send.at[which, g, mask], small_recv.at[which, g, mask],
        )

    def ys_copy(k):
        return to_row(
            0, small.at[pl.ds(1, 2), k], pair_ys.at[odd, :, k], ys_send.at[k], ys_recv.at[k]
        )

    def s_copy(level, k):
        return to_row(
            level, pair_ys.at[0, 1, k], pair_s.at[level, k],
            s_send.at[level, k], s_recv.at[level, k],
        )

    def vb_copy(k):
        there = pair_vb.at[odd, k]
        return to_row(0, there, there, vb_send.at[k], vb_recv.at[k])

    def top_copy():
        return to_row(0, top_out.at[other], tops.at[odd], top_send, top_recv)

    def r_copy(k, p):
        return to_row(
            0, r_all.at[k, other, p], r_got.at[k, p], r_send.at[k, p], r_recv.at[k, p]
        )

    def w_copy(k):
        return to_row(0, w_out.at[k], w_got.at[k], w_send.at[k], w_recv.at[k])

    def t_copy(k, level, p):
        return to_row(
            level, sent.at[k, level, p], got.at[k, level, p],
            t_send.at[k, level, p], t_recv.at[k, level, p],
        )

    def b_copy(p):
        return to_row(0, b_out.at[p], b_got.at[p], b_send.at[p], b_recv.at[p])

    def is_lower(level):
        return node_of % (2 << level) == 1 << level

    def is_upper(level):
        return node_of % (2 << level) == 0

    def takes_part(level):
        return node_of % (1 << level) == 0

    def ends_at(level):
        return takes_part(level) if level == levels - 1 else is_lower(level)

    masks = range(1, n_col)
    near = [mask for mask in masks if mask == 1]
    far = [mask for mask in masks if mask > 1 and mask == low_bit(mask)]
    relayed = [mask for mask in masks if mask != low_bit(mask)]

    barrier = pltpu.get_barrier_semaphore()
    for mask in masks:
        pl.semaphore_signal(
            barrier, inc=1, device_id={"row": r, "col": partner(mask)}, device_id_type=MESH
        )
    for level in range(levels):
        pl.semaphore_signal(
            barrier, inc=1, device_id={"row": row_partner(level), "col": c}, device_id_type=MESH
        )

    a_copy(0).start()
    v_own(0).start()
    for mask in masks:
        a_copy(mask).start()
    for g in range(len(groups)):
        for which in range(3):
            small_local(which, g).start()
    for k in range(1, panels):
        v_own(k).start()

    pl.semaphore_wait(barrier, n_col - 1 + levels)

    for k in range(panels):
        if k < len(groups):
            for mask in far + near:
                for which in range(3):
                    small_copy(which, k, mask).start()
        for mask in far + near:
            for p in range(len(cuts(mask))):
                v_copy(k, mask, p).start()

    def project(k, mask, first, last):
        base = block_start(mask)
        wide = cols + k * width

        def step(t, carry_in):
            start = pl.multiple_of(base + t * TILE, TILE)
            at = pl.ds(start, TILE)
            row = lax.broadcasted_iota(jnp.int32, (TILE, width), 0) + start
            high, low = split(jnp.where(row >= width, v[k, at], 0.0))
            both = jnp.concatenate([high, low], axis=1)
            a_high, a_low = split(a[at, :])
            before = [vc[at, 2 * width * j:2 * width * (j + 1)] for j in range(k)]
            right = jnp.concatenate([a_high] + [x[:, :width] for x in before], axis=1)
            right_low = jnp.concatenate([a_low] + [x[:, width:] for x in before], axis=1)
            vc[at, 2 * width * k:2 * width * (k + 1)] = both
            out = mm(both, right, 0)
            q[k, :, :wide] += out[:width] + out[width:] + mm(high, right_low, 0)
            return carry_in

        lax.fori_loop(first, last, step, 0)

    def update(ks, first, last):
        terms = [(2 * width * k, 2 * width) for k in ks]
        low_terms = [2 * width * panels + width * k for k in ks]

        def step(t, carry_in):
            at = pl.ds(pl.multiple_of(t * UPDATE, UPDATE), UPDATE)
            left = jnp.concatenate(
                [vc[at, first_col:first_col + size] for first_col, size in terms]
                + [vc[at, first_col:first_col + width] for first_col, size in terms],
                axis=1,
            )
            right = jnp.concatenate([
                jnp.concatenate(
                    [w_all[h, row:row + size, :] for row, size in terms]
                    + [w_all[h, row:row + width, :] for row in low_terms],
                    axis=0,
                )
                for h in range(2)
            ], axis=1)
            a[at, :] = a[at, :] - mm(left, right, 1)
            return carry_in

        lax.fori_loop(first, last, step, 0)

    def make_vb(k):
        head = v[k, pl.ds(0, width)]
        pair_vb[odd, k, 0] = head
        pair_vb[odd, k, 1] = dot3(head, upper_triangle(small[0, k]), 1)
        vb_copy(k).start()

    def set_w(k, h, w):
        high, low = split(w)
        w_all[h, 2 * width * k:2 * width * k + width, :] = high
        w_all[h, 2 * width * k + width:2 * width * (k + 1), :] = high
        w_all[h, 2 * width * panels + width * k:2 * width * panels + width * (k + 1), :] = low

    def make_r(k):
        proj = q[k, :, :cols]
        if k:
            w_before = tuple(
                jnp.concatenate(
                    [
                        jnp.concatenate([w_all[h, at:at + width, :] for h in range(2)], axis=1)
                        for at in range(first, first + step * k, step)
                    ],
                    axis=0,
                )
                for first, step in ((0, 2 * width), (2 * width * panels, width))
            )
            proj -= dot3(q[k, :, cols:cols + width * k], w_before, 1)
        out = dot3(upper_triangle(small[0, k]), proj, 0)
        for p in range(half):
            for h in range(2):
                at = h * span + p * CHUNK
                r_all[k, h, p] = out[:, at:at + CHUNK]
            r_copy(k, p).start()

    def plan(k):
        vb_copy(k).wait_recv()
        head = pair_vb[0, k, 0]
        lower = dot3(pair_ys[1, 0, k], pair_vb[1, k, 0], 0)
        coupled = couple(pair_ys[1, 1, k], jnp.concatenate([head, lower], axis=1))
        both = jnp.concatenate([head, jnp.zeros_like(head)], axis=1) - coupled
        step_m[k, 0] = both
        step_m[k, 1] = dot3(pair_ys[0, 0, k], both, 0)

    def before(k):
        x = tops[0]
        x_lower = tops[1]
        pre_w[0] = dot3(pair_vb[0, k, 1], x, 0)
        pre_w[1] = dot3(pair_vb[1, k, 1], x_lower, 0)
        after = x - couple(pair_ys[1, 1, k], x + dot3(pair_ys[1, 0, k], x_lower, 0))
        pre_x[...] = after
        if levels > 1:
            @pl.when(is_lower(1))
            def _():
                pre_z[...] = dot3(pair_ys[0, 0, k], after, 0)

    def take_w(k):
        w_copy(k).wait_recv()
        set_w(k, other, w_got[k])

    def couple(s, total):
        return dot3(upper_triangle(s), total, 0)

    def piece(p):
        return slice(p * CHUNK, (p + 1) * CHUNK)

    def first_level(k, final):
        for p in range(half):
            r_copy(k, p).wait_recv()
            w_pair[odd, p] = r_all[k, odd, p] + pre_w[odd, :, piece(p)]
            w_pair[other, p] = r_got[k, p] + pre_w[other, :, piece(p)]
            w = split(jnp.concatenate([w_pair[0, p], w_pair[1, p]], axis=0))
            if levels == 1:
                carry[p] = pre_x[:, piece(p)] - dot3(step_m[k, 0], w, 1)
                end_level(final, 0, p)
                continue

            @pl.when(is_lower(1))
            def _():
                sent[k, 1, p] = pre_z[:, piece(p)] - dot3(step_m[k, 1], w, 1)
                t_copy(k, 1, p).start()
                carry[p] = pre_x[:, piece(p)] - dot3(step_m[k, 0], w, 1)

            @pl.when(is_upper(1))
            def _():
                upper = pre_x[:, piece(p)] - dot3(step_m[k, 0], w, 1)
                carry[p] = upper
                sent[k, 1, p] = upper
                t_copy(k, 1, p).start()

        for p in range(half):
            w_out[k, :, piece(p)] = w_pair[other, p]
        w_copy(k).start()

        def joined(ref, *index):
            return jnp.concatenate([ref[(*index, p)] for p in range(half)], axis=1)

        set_w(k, odd, joined(w_pair, odd))
        x = tops[0] - dot3(pair_vb[0, k, 0], joined(w_pair, 0), 1)
        x_lower = tops[1] - dot3(pair_vb[1, k, 0], joined(w_pair, 1), 1)
        x_lower -= dot3(pair_ys[1, 0, k], x - joined(carry), 1)
        tops[1] = x_lower

        if final:
            @pl.when(is_even)
            def _():
                for p in range(half):
                    b_out[p] = x_lower[:, piece(p)]
                    b_copy(p).start()

    def send_level(k, level, p):
        @pl.when(is_lower(level))
        def _():
            sent[k, level, p] = dot3(pair_ys[0, 0, k], carry[p], 0)

        @pl.when(is_upper(level))
        def _():
            sent[k, level, p] = carry[p]

        @pl.when(takes_part(level))
        def _():
            t_copy(k, level, p).start()

    def take_level(k, level, p):
        @pl.when(takes_part(level))
        def _():
            t_copy(k, level, p).wait_recv()
            coupled = couple(pair_s[level, k], sent[k, level, p] + got[k, level, p])

            @pl.when(is_lower(level))
            def _():
                carry[p] -= dot3(pair_ys[0, 0, k], coupled, 1)

            @pl.when(is_upper(level))
            def _():
                carry[p] -= coupled

    def end_level(final, level, p):
        if final:
            @pl.when(ends_at(level) & is_odd)
            def _():
                b_out[p] = carry[p]
                b_copy(p).start()

    def pass_on(mask):
        bit = 1
        while bit < low_bit(mask):
            yield mask | bit
            bit *= 2

    def small_far(g):
        for mask in near + far:
            for which in range(3):
                small_copy(which, g, mask).wait_recv()
                for onward in pass_on(mask):
                    small_copy(which, g, onward).start()

    def small_rest(g):
        for mask in relayed:
            for which in range(3):
                small_copy(which, g, mask).wait_recv()
                for onward in pass_on(mask):
                    small_copy(which, g, onward).start()
        for which in range(3):
            small_local(which, g).wait()

    def share_ys(k):
        ys_copy(k).start()
        pair_ys[odd, :, k] = small[pl.ds(1, 2), k]

    def node_rest(k):
        ys_copy(k).wait_recv()
        for level in range(1, levels):
            @pl.when(is_lower(level))
            def _():
                s_copy(level, k).start()
                pair_s[level, k] = pair_ys[0, 1, k]

    def pair_rest(k):
        for level in range(1, levels):
            @pl.when(is_upper(level))
            def _():
                s_copy(level, k).wait_recv()

    def receive(k, mask, p):
        v_copy(k, mask, p).wait_recv()
        for onward in pass_on(mask):
            v_copy(k, onward, p).start()

    steps = shard // TILE
    per_step = TILE // PIECE

    def far_step(k, t):
        for mask in far + relayed:
            for p in range(per_step * t, per_step * (t + 1)):
                receive(k, mask, p)
            project(k, mask, t, t + 1)

    def near_all(k):
        v_own(k).wait()
        project(k, 0, 0, steps)
        for mask in near:
            receive(k, mask, 0)
            project(k, mask, 0, steps)

    def far_all(k, t):
        far_step(k, t)
        if t == 0:
            make_vb(k)
        if t == steps - 1:
            make_r(k)

    def sent_inputs():
        for k in range(panels):
            for mask in masks:
                for p in range(len(cuts(mask))):
                    v_copy(k, mask, p).wait_send()
            ys_copy(k).wait_send()
            for level in range(1, levels):
                @pl.when(is_lower(level))
                def _():
                    s_copy(level, k).wait_send()

            vb_copy(k).wait_send()
        for g in range(len(groups)):
            for which in range(3):
                for mask in masks:
                    small_copy(which, g, mask).wait_send()
        top_copy().wait_send()

    def sent_panel(k):
        for p in range(half):
            r_copy(k, p).wait_send()
        w_copy(k).wait_send()
        for level in range(1, levels):
            @pl.when(takes_part(level))
            def _():
                for p in range(half):
                    t_copy(k, level, p).wait_send()

    def finish_sends():
        sent_inputs()
        for k in range(panels - 1):
            sent_panel(k)

    q[...] = jnp.zeros_like(q)
    for mask in range(n_col):
        a_copy(mask).wait()
    top_out[0] = a[:width, :span]
    top_out[1] = a[:width, span:]
    top_copy().start()
    tops[odd] = top_out[odd]
    near_all(0)
    small_far(0)
    small_rest(0)
    share_ys(0)
    for k in range(1, panels):
        near_all(k)
    for t in range(steps):
        far_all(0, t)
    node_rest(0)
    top_copy().wait_recv()
    plan(0)

    for k in range(panels):
        final = k == panels - 1

        def next_vectors(first, last):
            if not final:
                for t in range(first, last):
                    far_all(k + 1, t)

        before(k)
        first_level(k, final)
        if not final:
            small_far(k + 1)
            small_rest(k + 1)
            share_ys(k + 1)
        next_vectors(0, steps - 1)
        if final and k > 0:
            update(range(k), 0, tiles * 3 // 4)
        pair_rest(k)
        for level in range(1, levels):
            for p in range(half):
                take_level(k, level, p)
                if level + 1 < levels:
                    send_level(k, level + 1, p)
                end_level(final, level, p)
            if level == 1:
                if final and k > 0:
                    update(range(k), tiles * 3 // 4, tiles)
                take_w(k)
                next_vectors(steps - 1, steps)
                if not final:
                    node_rest(k + 1)
                    plan(k + 1)
                else:
                    update([k], 0, tiles)
                    finish_sends()
        if levels == 1:
            if final and k > 0:
                update(range(k), tiles * 3 // 4, tiles)
            take_w(k)
            next_vectors(steps - 1, steps)
            if not final:
                node_rest(k + 1)
                plan(k + 1)
            else:
                update([k], 0, tiles)
                finish_sends()
        for p in range(half):
            tops[0, :, piece(p)] = carry[p]

    for p in range(half):
        b_copy(p).wait_recv()

    @pl.when(is_even)
    def _():
        a[:width, :span] = tops[0]
        for p in range(half):
            a[:width, span + p * CHUNK:span + (p + 1) * CHUNK] = b_got[p]

    @pl.when(is_odd)
    def _():
        a[:width, span:] = tops[1]
        for p in range(half):
            a[:width, p * CHUNK:(p + 1) * CHUNK] = b_got[p]

    sent_panel(panels - 1)
    for p in range(half):
        b_copy(p).wait_send()


def local(n_row, n_col, matrix, leaf_vectors, leaf_factors, tree_vectors, tree_factors):
    rows, cols = matrix.shape
    panels, shard, width = leaf_vectors.shape
    levels = n_row.bit_length() - 1
    pieces = shard // PIECE
    span = cols // 2
    half = span // CHUNK
    groups = panels
    dma = pltpu.SemaphoreType.DMA
    vmem = pltpu.VMEM
    return pl.pallas_call(
        functools.partial(kernel, n_row, n_col),
        out_shape=pltpu.VMEM((rows, cols), F32),
        in_specs=[pl.BlockSpec(memory_space=pltpu.HBM)] * 5,
        out_specs=pl.BlockSpec(memory_space=pltpu.VMEM),
        scratch_shapes=[
            vmem((panels, rows, width), F32),
            vmem((rows, 2 * width * panels), BF16),
            vmem((3, panels, width, width), F32),
            vmem((2, 2, panels, width, width), F32),
            vmem((levels, panels, width, width), F32),
            vmem((2, panels, 2, width, width), F32),
            vmem((2, width, span), F32),
            vmem((2, width, span), F32),
            vmem((half, width, CHUNK), F32),
            vmem((panels, width, cols + width * (panels - 1)), F32),
            vmem((2, 3 * width * panels, span), BF16),
            vmem((panels, 2, half, width, CHUNK), F32),
            vmem((panels, half, width, CHUNK), F32),
            vmem((2, half, width, CHUNK), F32),
            vmem((panels, width, span), F32),
            vmem((panels, width, span), F32),
            vmem((2, width, span), F32),
            vmem((width, span), F32),
            vmem((width, span), F32),
            vmem((panels, 2, width, 2 * width), F32),
            vmem((panels, levels, half, width, CHUNK), F32),
            vmem((panels, levels, half, width, CHUNK), F32),
            vmem((half, width, CHUNK), F32),
            vmem((half, width, CHUNK), F32),
            dma((n_col,)),
            dma((panels,)),
            dma((panels, n_col, pieces)),
            dma((panels, n_col, pieces)),
            dma((3, groups)),
            dma((3, groups, n_col)),
            dma((3, groups, n_col)),
            dma((panels,)),
            dma((panels,)),
            dma((levels, panels)),
            dma((levels, panels)),
            dma((panels,)),
            dma((panels,)),
            dma(()),
            dma(()),
            dma((panels, half)),
            dma((panels, half)),
            dma((panels,)),
            dma((panels,)),
            dma((panels, levels, half)),
            dma((panels, levels, half)),
            dma((half,)),
            dma((half,)),
        ],
        compiler_params=pltpu.CompilerParams(
            collective_id=0, has_side_effects=True, vmem_limit_bytes=48 << 20
        ),
    )(matrix, leaf_vectors, leaf_factors, tree_vectors, tree_factors)


def solution(mesh):
    placed = (
        P("row", "col"),
        P(None, ("row", "col"), None),
        P(None, ("row", "col"), None),
        P(None, ("row", "col"), None),
        P(None, ("row", "col"), None),
    )
    return jax.shard_map(
        functools.partial(local, mesh.shape["row"], mesh.shape["col"]),
        mesh=mesh, in_specs=placed, out_specs=P("row", "col"), check_vma=False,
    )
```

```python
import functools

import jax
import jax.numpy as jnp
from jax import lax
from jax.experimental import pallas as pl
from jax.experimental.pallas import tpu as pltpu
from jax.sharding import PartitionSpec as P

MESH = pl.DeviceIdType.MESH
F32 = jnp.float32
BF16 = jnp.bfloat16
TILE = 512
UPDATE = 1024
PIECE = 512
CHUNK = 128


def split(x):
    high = x.astype(BF16)
    return high, (x - high.astype(F32)).astype(BF16)


def mm(x, y, contract_x):
    return lax.dot_general(
        x, y, (((contract_x,), (0,)), ((), ())), preferred_element_type=F32
    )


def dot3(x, y, contract_x):
    x_high, x_low = x if isinstance(x, tuple) else split(x)
    y_high, y_low = y if isinstance(y, tuple) else split(y)
    return (
        mm(x_high, y_high, contract_x)
        + mm(x_low, y_high, contract_x)
        + mm(x_high, y_low, contract_x)
    )


def upper_triangle(x):
    row = lax.broadcasted_iota(jnp.int32, x.shape, 0)
    col = lax.broadcasted_iota(jnp.int32, x.shape, 1)
    return jnp.where(row <= col, x, 0.0)


def low_bit(mask):
    return mask & -mask


def kernel(
    n_row, n_col,
    a_in, v_in, l_in, y_in, s_in, a,
    v, vc, small, pair_ys, pair_s, pair_vb, top_out, tops, carry, q, w_all,
    r_all, r_got, w_pair, w_out, w_got, pre_w, pre_x, pre_y, pre_z, step_m,
    sent, got, b_out, b_got,
    a_sem, v_own_sem, v_send, v_recv, small_own, small_send, small_recv,
    ys_send, ys_recv, s_send, s_recv, vb_send, vb_recv, top_send, top_recv,
    r_send, r_recv, w_send, w_recv, t_send, t_recv, b_send, b_recv,
):
    panels, shard, width = v_in.shape
    rows, cols = a_in.shape
    part = l_in.shape[1]
    levels = n_row.bit_length() - 1
    tiles = rows // UPDATE
    pieces = shard // PIECE
    span = cols // 2
    half = span // CHUNK
    r = lax.axis_index("row")
    c = lax.axis_index("col")
    odd = r % 2
    other = 1 - odd
    node_of = r - odd
    is_even = odd == 0
    is_odd = odd == 1
    groups = [(k, 1) for k in range(panels)]

    def partner(mask):
        bits = c
        for bit in range(n_col.bit_length() - 1):
            if mask >> bit & 1:
                bits = bits + (1 << bit) - 2 * (1 << bit) * ((bits // (1 << bit)) % 2)
        return bits

    def row_partner(level):
        step = 1 << level
        return r + step - 2 * step * ((r // step) % 2)

    def block_start(mask):
        return pl.multiple_of(partner(mask) * shard, shard)

    def part_rows(mask):
        return pl.ds(pl.multiple_of(partner(mask) * part, part), part)

    def to_row(level, source, there, send, recv):
        return pltpu.make_async_remote_copy(
            src_ref=source, dst_ref=there, send_sem=send, recv_sem=recv,
            device_id={"row": row_partner(level), "col": c}, device_id_type=MESH,
        )

    def to_col(bit, source, there, send, recv):
        return pltpu.make_async_remote_copy(
            src_ref=source, dst_ref=there, send_sem=send, recv_sem=recv,
            device_id={"row": r, "col": partner(bit)}, device_id_type=MESH,
        )

    def a_copy(mask):
        at = pl.ds(block_start(mask), shard)
        return pltpu.make_async_copy(a_in.at[at], a.at[at], a_sem.at[mask])

    def v_own(k):
        at = pl.ds(block_start(0), shard)
        return pltpu.make_async_copy(v_in.at[k], v.at[k, at], v_own_sem.at[k])

    def cuts(mask):
        return [(0, shard)] if mask == 1 else [(p * PIECE, PIECE) for p in range(pieces)]

    def v_copy(k, mask, p):
        first, size = cuts(mask)[p]
        bit = low_bit(mask)
        held = mask ^ bit
        there = v.at[k, pl.ds(block_start(held) + first, size)]
        source = v_in.at[k, pl.ds(first, size)] if held == 0 else there
        return to_col(bit, source, there, v_send.at[k, mask, p], v_recv.at[k, mask, p])

    small_in = (l_in, y_in, s_in)

    def small_local(which, g):
        k = pl.ds(*groups[g])
        return pltpu.make_async_copy(
            small_in[which].at[k], small.at[which, k, part_rows(0)], small_own.at[which, g]
        )

    def small_copy(which, g, mask):
        bit = low_bit(mask)
        held = mask ^ bit
        k = pl.ds(*groups[g])
        there = small.at[which, k, part_rows(held)]
        return to_col(
            bit, small_in[which].at[k] if held == 0 else there, there,
            small_send.at[which, g, mask], small_recv.at[which, g, mask],
        )

    def ys_copy(k):
        return to_row(
            0, small.at[pl.ds(1, 2), k], pair_ys.at[odd, :, k], ys_send.at[k], ys_recv.at[k]
        )

    def s_copy(level, k):
        return to_row(
            level, pair_ys.at[0, 1, k], pair_s.at[level, k],
            s_send.at[level, k], s_recv.at[level, k],
        )

    def vb_copy(k):
        there = pair_vb.at[odd, k]
        return to_row(0, there, there, vb_send.at[k], vb_recv.at[k])

    def top_copy():
        return to_row(0, top_out.at[other], tops.at[odd], top_send, top_recv)

    def r_copy(k, p):
        return to_row(
            0, r_all.at[k, other, p], r_got.at[k, p], r_send.at[k, p], r_recv.at[k, p]
        )

    def w_copy(k):
        return to_row(0, w_out.at[k], w_got.at[k], w_send.at[k], w_recv.at[k])

    def t_copy(k, level, p):
        return to_row(
            level, sent.at[k, level, p], got.at[k, level, p],
            t_send.at[k, level, p], t_recv.at[k, level, p],
        )

    def b_copy(p):
        return to_row(0, b_out.at[p], b_got.at[p], b_send.at[p], b_recv.at[p])

    def is_lower(level):
        return node_of % (2 << level) == 1 << level

    def is_upper(level):
        return node_of % (2 << level) == 0

    def takes_part(level):
        return node_of % (1 << level) == 0

    def ends_at(level):
        return takes_part(level) if level == levels - 1 else is_lower(level)

    masks = range(1, n_col)
    near = [mask for mask in masks if mask == 1]
    far = [mask for mask in masks if mask > 1 and mask == low_bit(mask)]
    relayed = [mask for mask in masks if mask != low_bit(mask)]

    barrier = pltpu.get_barrier_semaphore()
    for mask in masks:
        pl.semaphore_signal(
            barrier, inc=1, device_id={"row": r, "col": partner(mask)}, device_id_type=MESH
        )
    for level in range(levels):
        pl.semaphore_signal(
            barrier, inc=1, device_id={"row": row_partner(level), "col": c}, device_id_type=MESH
        )

    a_copy(0).start()
    v_own(0).start()
    for mask in masks:
        a_copy(mask).start()
    for g in range(len(groups)):
        for which in range(3):
            small_local(which, g).start()
    for k in range(1, panels):
        v_own(k).start()

    pl.semaphore_wait(barrier, n_col - 1 + levels)

    for k in range(panels):
        if k < len(groups):
            for mask in far + near:
                for which in range(3):
                    small_copy(which, k, mask).start()
        for mask in far + near:
            for p in range(len(cuts(mask))):
                v_copy(k, mask, p).start()

    def project(k, mask, first, last):
        base = block_start(mask)
        wide = cols + k * width

        def step(t, carry_in):
            start = pl.multiple_of(base + t * TILE, TILE)
            at = pl.ds(start, TILE)
            row = lax.broadcasted_iota(jnp.int32, (TILE, width), 0) + start
            high, low = split(jnp.where(row >= width, v[k, at], 0.0))
            both = jnp.concatenate([high, low], axis=1)
            a_high, a_low = split(a[at, :])
            before = [vc[at, 2 * width * j:2 * width * (j + 1)] for j in range(k)]
            right = jnp.concatenate([a_high] + [x[:, :width] for x in before], axis=1)
            right_low = jnp.concatenate([a_low] + [x[:, width:] for x in before], axis=1)
            vc[at, 2 * width * k:2 * width * (k + 1)] = both
            out = mm(both, right, 0)
            q[k, :, :wide] += out[:width] + out[width:] + mm(high, right_low, 0)
            return carry_in

        lax.fori_loop(first, last, step, 0)

    def update(ks, first, last):
        terms = [(2 * width * k, 2 * width) for k in ks]
        low_terms = [2 * width * panels + width * k for k in ks]

        def step(t, carry_in):
            at = pl.ds(pl.multiple_of(t * UPDATE, UPDATE), UPDATE)
            left = jnp.concatenate(
                [vc[at, first_col:first_col + size] for first_col, size in terms]
                + [vc[at, first_col:first_col + width] for first_col, size in terms],
                axis=1,
            )
            right = jnp.concatenate([
                jnp.concatenate(
                    [w_all[h, row:row + size, :] for row, size in terms]
                    + [w_all[h, row:row + width, :] for row in low_terms],
                    axis=0,
                )
                for h in range(2)
            ], axis=1)
            a[at, :] = a[at, :] - mm(left, right, 1)
            return carry_in

        lax.fori_loop(first, last, step, 0)

    def make_vb(k):
        head = v[k, pl.ds(0, width)]
        pair_vb[odd, k, 0] = head
        pair_vb[odd, k, 1] = dot3(head, upper_triangle(small[0, k]), 1)
        vb_copy(k).start()

    def set_w(k, h, w):
        high, low = split(w)
        w_all[h, 2 * width * k:2 * width * k + width, :] = high
        w_all[h, 2 * width * k + width:2 * width * (k + 1), :] = high
        w_all[h, 2 * width * panels + width * k:2 * width * panels + width * (k + 1), :] = low

    def make_r(k):
        proj = q[k, :, :cols]
        if k:
            w_before = tuple(
                jnp.concatenate(
                    [
                        jnp.concatenate([w_all[h, at:at + width, :] for h in range(2)], axis=1)
                        for at in range(first, first + step * k, step)
                    ],
                    axis=0,
                )
                for first, step in ((0, 2 * width), (2 * width * panels, width))
            )
            proj -= dot3(q[k, :, cols:cols + width * k], w_before, 1)
        out = dot3(upper_triangle(small[0, k]), proj, 0)
        for p in range(half):
            for h in range(2):
                at = h * span + p * CHUNK
                r_all[k, h, p] = out[:, at:at + CHUNK]
            r_copy(k, p).start()

    def plan(k):
        vb_copy(k).wait_recv()
        head = pair_vb[0, k, 0]
        lower = dot3(pair_ys[1, 0, k], pair_vb[1, k, 0], 0)
        coupled = couple(pair_ys[1, 1, k], jnp.concatenate([head, lower], axis=1))
        both = jnp.concatenate([head, jnp.zeros_like(head)], axis=1) - coupled
        step_m[k, 0] = both
        step_m[k, 1] = dot3(pair_ys[0, 0, k], both, 0)

    def before_lower(k):
        x_lower = tops[1]
        pre_w[1] = dot3(pair_vb[1, k, 1], x_lower, 0)
        pre_y[...] = dot3(pair_ys[1, 0, k], x_lower, 0)

    def before(k):
        x = tops[0]
        pre_w[0] = dot3(pair_vb[0, k, 1], x, 0)
        after = x - couple(pair_ys[1, 1, k], x + pre_y[...])
        pre_x[...] = after
        if levels > 1:
            @pl.when(is_lower(1))
            def _():
                pre_z[...] = dot3(pair_ys[0, 0, k], after, 0)

    def take_w(k):
        w_copy(k).wait_recv()
        set_w(k, other, w_got[k])

    def couple(s, total):
        return dot3(upper_triangle(s), total, 0)

    def piece(p):
        return slice(p * CHUNK, (p + 1) * CHUNK)

    def first_level(k, final):
        for p in range(half):
            r_copy(k, p).wait_recv()
            w_pair[odd, p] = r_all[k, odd, p] + pre_w[odd, :, piece(p)]
            w_pair[other, p] = r_got[k, p] + pre_w[other, :, piece(p)]
            w = split(jnp.concatenate([w_pair[0, p], w_pair[1, p]], axis=0))
            if levels == 1:
                carry[p] = pre_x[:, piece(p)] - dot3(step_m[k, 0], w, 1)
                end_level(final, 0, p)
                continue

            @pl.when(is_lower(1))
            def _():
                sent[k, 1, p] = pre_z[:, piece(p)] - dot3(step_m[k, 1], w, 1)
                t_copy(k, 1, p).start()
                carry[p] = pre_x[:, piece(p)] - dot3(step_m[k, 0], w, 1)

            @pl.when(is_upper(1))
            def _():
                upper = pre_x[:, piece(p)] - dot3(step_m[k, 0], w, 1)
                carry[p] = upper
                sent[k, 1, p] = upper
                t_copy(k, 1, p).start()

        for p in range(half):
            w_out[k, :, piece(p)] = w_pair[other, p]
        w_copy(k).start()

        def joined(ref, *index):
            return jnp.concatenate([ref[(*index, p)] for p in range(half)], axis=1)

        set_w(k, odd, joined(w_pair, odd))
        x = tops[0] - dot3(pair_vb[0, k, 0], joined(w_pair, 0), 1)
        x_lower = tops[1] - dot3(pair_vb[1, k, 0], joined(w_pair, 1), 1)
        x_lower -= dot3(pair_ys[1, 0, k], x - joined(carry), 1)
        tops[1] = x_lower

        if final:
            @pl.when(is_even)
            def _():
                for p in range(half):
                    b_out[p] = x_lower[:, piece(p)]
                    b_copy(p).start()

    def send_level(k, level, p):
        @pl.when(is_lower(level))
        def _():
            sent[k, level, p] = dot3(pair_ys[0, 0, k], carry[p], 0)

        @pl.when(is_upper(level))
        def _():
            sent[k, level, p] = carry[p]

        @pl.when(takes_part(level))
        def _():
            t_copy(k, level, p).start()

    def take_level(k, level, p):
        @pl.when(takes_part(level))
        def _():
            t_copy(k, level, p).wait_recv()
            coupled = couple(pair_s[level, k], sent[k, level, p] + got[k, level, p])

            @pl.when(is_lower(level))
            def _():
                carry[p] -= dot3(pair_ys[0, 0, k], coupled, 1)

            @pl.when(is_upper(level))
            def _():
                carry[p] -= coupled

    def end_level(final, level, p):
        if final:
            @pl.when(ends_at(level) & is_odd)
            def _():
                b_out[p] = carry[p]
                b_copy(p).start()

    def pass_on(mask):
        bit = 1
        while bit < low_bit(mask):
            yield mask | bit
            bit *= 2

    def small_far(g):
        for mask in near + far:
            for which in range(3):
                small_copy(which, g, mask).wait_recv()
                for onward in pass_on(mask):
                    small_copy(which, g, onward).start()

    def small_rest(g):
        for mask in relayed:
            for which in range(3):
                small_copy(which, g, mask).wait_recv()
                for onward in pass_on(mask):
                    small_copy(which, g, onward).start()
        for which in range(3):
            small_local(which, g).wait()

    def share_ys(k):
        ys_copy(k).start()
        pair_ys[odd, :, k] = small[pl.ds(1, 2), k]

    def node_rest(k):
        ys_copy(k).wait_recv()
        for level in range(1, levels):
            @pl.when(is_lower(level))
            def _():
                s_copy(level, k).start()
                pair_s[level, k] = pair_ys[0, 1, k]

    def pair_rest(k):
        for level in range(1, levels):
            @pl.when(is_upper(level))
            def _():
                s_copy(level, k).wait_recv()

    def receive(k, mask, p):
        v_copy(k, mask, p).wait_recv()
        for onward in pass_on(mask):
            v_copy(k, onward, p).start()

    steps = shard // TILE
    per_step = TILE // PIECE

    def far_step(k, t):
        for mask in far + relayed:
            for p in range(per_step * t, per_step * (t + 1)):
                receive(k, mask, p)
            project(k, mask, t, t + 1)

    def near_all(k):
        v_own(k).wait()
        project(k, 0, 0, steps)
        for mask in near:
            receive(k, mask, 0)
            project(k, mask, 0, steps)

    def far_all(k, t):
        far_step(k, t)
        if t == 0:
            make_vb(k)
        if t == steps - 1:
            make_r(k)

    def sent_inputs():
        for k in range(panels):
            for mask in masks:
                for p in range(len(cuts(mask))):
                    v_copy(k, mask, p).wait_send()
            ys_copy(k).wait_send()
            for level in range(1, levels):
                @pl.when(is_lower(level))
                def _():
                    s_copy(level, k).wait_send()

            vb_copy(k).wait_send()
        for g in range(len(groups)):
            for which in range(3):
                for mask in masks:
                    small_copy(which, g, mask).wait_send()
        top_copy().wait_send()

    def sent_panel(k):
        for p in range(half):
            r_copy(k, p).wait_send()
        w_copy(k).wait_send()
        for level in range(1, levels):
            @pl.when(takes_part(level))
            def _():
                for p in range(half):
                    t_copy(k, level, p).wait_send()

    def finish_sends():
        sent_inputs()
        for k in range(panels - 1):
            sent_panel(k)

    q[...] = jnp.zeros_like(q)
    for mask in range(n_col):
        a_copy(mask).wait()
    top_out[0] = a[:width, :span]
    top_out[1] = a[:width, span:]
    top_copy().start()
    tops[odd] = top_out[odd]
    near_all(0)
    small_far(0)
    small_rest(0)
    share_ys(0)
    for k in range(1, panels):
        near_all(k)
    for t in range(steps):
        far_all(0, t)
    node_rest(0)
    top_copy().wait_recv()
    plan(0)
    before_lower(0)

    for k in range(panels):
        final = k == panels - 1

        def next_vectors(first, last):
            if not final:
                for t in range(first, last):
                    far_all(k + 1, t)

        before(k)
        first_level(k, final)
        if not final:
            small_far(k + 1)
            small_rest(k + 1)
            share_ys(k + 1)
        next_vectors(0, steps - 1)
        if final and k > 0:
            update(range(k), 0, tiles * 3 // 4)
        pair_rest(k)
        for level in range(1, levels):
            for p in range(half):
                take_level(k, level, p)
                if level + 1 < levels:
                    send_level(k, level + 1, p)
                end_level(final, level, p)
            if level == 1:
                if final and k > 0:
                    update(range(k), tiles * 3 // 4, tiles)
                take_w(k)
                next_vectors(steps - 1, steps)
                if not final:
                    node_rest(k + 1)
                    plan(k + 1)
                    before_lower(k + 1)
                else:
                    update([k], 0, tiles)
                    finish_sends()
        if levels == 1:
            if final and k > 0:
                update(range(k), tiles * 3 // 4, tiles)
            take_w(k)
            next_vectors(steps - 1, steps)
            if not final:
                node_rest(k + 1)
                plan(k + 1)
                before_lower(k + 1)
            else:
                update([k], 0, tiles)
                finish_sends()
        for p in range(half):
            tops[0, :, piece(p)] = carry[p]

    for p in range(half):
        b_copy(p).wait_recv()

    @pl.when(is_even)
    def _():
        a[:width, :span] = tops[0]
        for p in range(half):
            a[:width, span + p * CHUNK:span + (p + 1) * CHUNK] = b_got[p]

    @pl.when(is_odd)
    def _():
        a[:width, span:] = tops[1]
        for p in range(half):
            a[:width, p * CHUNK:(p + 1) * CHUNK] = b_got[p]

    sent_panel(panels - 1)
    for p in range(half):
        b_copy(p).wait_send()


def local(n_row, n_col, matrix, leaf_vectors, leaf_factors, tree_vectors, tree_factors):
    rows, cols = matrix.shape
    panels, shard, width = leaf_vectors.shape
    levels = n_row.bit_length() - 1
    pieces = shard // PIECE
    span = cols // 2
    half = span // CHUNK
    groups = panels
    dma = pltpu.SemaphoreType.DMA
    vmem = pltpu.VMEM
    return pl.pallas_call(
        functools.partial(kernel, n_row, n_col),
        out_shape=pltpu.VMEM((rows, cols), F32),
        in_specs=[pl.BlockSpec(memory_space=pltpu.HBM)] * 5,
        out_specs=pl.BlockSpec(memory_space=pltpu.VMEM),
        scratch_shapes=[
            vmem((panels, rows, width), F32),
            vmem((rows, 2 * width * panels), BF16),
            vmem((3, panels, width, width), F32),
            vmem((2, 2, panels, width, width), F32),
            vmem((levels, panels, width, width), F32),
            vmem((2, panels, 2, width, width), F32),
            vmem((2, width, span), F32),
            vmem((2, width, span), F32),
            vmem((half, width, CHUNK), F32),
            vmem((panels, width, cols + width * (panels - 1)), F32),
            vmem((2, 3 * width * panels, span), BF16),
            vmem((panels, 2, half, width, CHUNK), F32),
            vmem((panels, half, width, CHUNK), F32),
            vmem((2, half, width, CHUNK), F32),
            vmem((panels, width, span), F32),
            vmem((panels, width, span), F32),
            vmem((2, width, span), F32),
            vmem((width, span), F32),
            vmem((width, span), F32),
            vmem((width, span), F32),
            vmem((panels, 2, width, 2 * width), F32),
            vmem((panels, levels, half, width, CHUNK), F32),
            vmem((panels, levels, half, width, CHUNK), F32),
            vmem((half, width, CHUNK), F32),
            vmem((half, width, CHUNK), F32),
            dma((n_col,)),
            dma((panels,)),
            dma((panels, n_col, pieces)),
            dma((panels, n_col, pieces)),
            dma((3, groups)),
            dma((3, groups, n_col)),
            dma((3, groups, n_col)),
            dma((panels,)),
            dma((panels,)),
            dma((levels, panels)),
            dma((levels, panels)),
            dma((panels,)),
            dma((panels,)),
            dma(()),
            dma(()),
            dma((panels, half)),
            dma((panels, half)),
            dma((panels,)),
            dma((panels,)),
            dma((panels, levels, half)),
            dma((panels, levels, half)),
            dma((half,)),
            dma((half,)),
        ],
        compiler_params=pltpu.CompilerParams(
            collective_id=0, has_side_effects=True, vmem_limit_bytes=48 << 20
        ),
    )(matrix, leaf_vectors, leaf_factors, tree_vectors, tree_factors)


def solution(mesh):
    placed = (
        P("row", "col"),
        P(None, ("row", "col"), None),
        P(None, ("row", "col"), None),
        P(None, ("row", "col"), None),
        P(None, ("row", "col"), None),
    )
    return jax.shard_map(
        functools.partial(local, mesh.shape["row"], mesh.shape["col"]),
        mesh=mesh, in_specs=placed, out_specs=P("row", "col"), check_vma=False,
    )
```
